32 devices in a mesh: groups: 2 (over y), ctx: 4 (over z), tp: 2 (over x), dp: 2 (over core).
Axes of the slice: x: 2, y: 2, z: 4, core: 2. Of those that a mesh axis runs over, the one named last changes fastest.
Arguments:
- hyena_in: bfloat16 [4, 576, 3, 8192], P(('groups', 'dp'), 'ctx', None, 'tp'), parts along dimension 0, may hold values from -6 to 6
- short_filter: bfloat16 [3, 7, 8192], P(None, None, 'tp'), may hold values from -2 to 2
- long_filter: bfloat16 [128, 512], P(None, 'tp'), may hold values from -0.5 to 0.5
- qkv: bfloat16 [4, 576, 3, 8192], P(('groups', 'dp'), 'ctx', None, 'tp'), parts along dimension 0, may hold values from -8 to 8
- lengths: int32 [4, 4], P(('groups', 'dp')), parts along dimension 0, may hold values from 1 to 432, 576 in all within a row
Outputs:
- hyena_out: bfloat16 [4, 576, 8192], P(('groups', 'dp'), 'ctx', 'tp'), parts along dimension 0
- attn_out: bfloat16 [4, 576, 8192], P(('groups', 'dp'), 'ctx', 'tp'), parts along dimension 0
The draws below stay inside these ranges and needn't reach their ends.
There are 2 independent parts, one for each index of `groups`. The reference program is written for one: setup_inputs(seed, part) draws one part's arguments, and reference() takes and returns one part's arrays. A program takes and returns all parts, laid end to end along the dimension named above; an argument that names none is the same for every part. Nothing has to cross between parts.
Inputs may be any that keep to these rules, and one draw needn't show every extreme that they name: Each stream is 4 packed sequences laid end to end from its first token, with lengths summing to 576; the longest is exactly 432.
All inputs are finite; a program needn't handle non-finite values.
Results may differ from the reference program's by a relative error of at most 0.005.
Values may be sent and summed in bfloat16 or wider, within the bound.
No kernel may reach another device: no remote copies, remote signals or barrier semaphores. Data moves between devices by JAX's collectives and lax.ppermute only.
A program may use at most 128 MiB of HBM per device.

```python
import math
import jax
import jax.numpy as jnp
import numpy as np
from jax import lax

D = 8192
NFILT = 512
H = 64
HD = 128
FILT = 128
SHORT = 7
NSEQ = 4
GROUP = 16
STREAMS = 2
LENGTH = 576


def draw_qkv(key, part):
    width = H * HD
    shape = (STREAMS, LENGTH, 3, width)
    base_key = jax.random.fold_in(key, 0)
    drawn = jax.random.normal(base_key, shape, jnp.float32)
    scales = jnp.array([2.5, 1.0, 1.0], jnp.float32)[None, None, :, None]
    return jnp.clip(drawn * scales, -8.0, 8.0).astype(jnp.bfloat16)


def block_levels(key, shape, pieces, low, high):
    level, own = 1.0, jax.random.fold_in(key, 6)
    for dim, parts in pieces:
        heights = jnp.exp(jax.random.uniform(jax.random.fold_in(own, dim), (parts,), jnp.float32, low / len(pieces), high / len(pieces)))
        level = level * jnp.repeat(heights, shape[dim] // parts).reshape([-1 if axis == dim else 1 for axis in range(len(shape))])
    return level


def split_up(amount, total, limit, slope):
    loads = [(1 << 20) // math.isqrt(grade ** slope) + 1 for grade in range(2, amount + 1)]
    rest, holding = total - limit - (amount - 1), [1] * (amount - 1)
    while rest > 0:
        movable = [i for i in range(amount - 1) if holding[i] < limit]
        whole, left = sum([loads[i] for i in movable]), rest
        for i in movable:
            extra = min(limit - holding[i], max(1, left * loads[i] // whole), rest)
            holding[i] = holding[i] + extra
            rest = rest - extra
    return np.array([limit] + holding)


def uneven(key, count, total, most, slope):
    if count == 2:
        one = jax.random.randint(key, (), max(1, total - most), min(most, total - 1) + 1)
        return jnp.stack([one, total - one])
    sizes = jnp.asarray(split_up(count, total, most, slope), jnp.int32)
    twos = (count - 1) // 2
    source_of, taker = sizes[1:1 + 2 * twos:2], sizes[2:2 + 2 * twos:2]
    margin = jnp.minimum(source_of - 1, most - taker)
    passed = jax.random.randint(jax.random.fold_in(key, 1), (twos,), 0, 1 << 20) % (margin + 1)
    sizes = sizes.at[1:1 + 2 * twos:2].set(source_of - passed).at[2:2 + 2 * twos:2].set(taker + passed)
    return sizes[jax.random.permutation(jax.random.fold_in(key, 2), count)]


def normal_values(rng, shape, scale, reach, cuts=(), kind=jnp.bfloat16):
    level = block_levels(rng, shape, cuts, -0.22, 0.18) if cuts else 1.0
    entries = jax.random.normal(rng, shape, jnp.float32) * scale * level
    return jnp.minimum(jnp.maximum(entries, -reach), reach).astype(kind)


def setup_inputs(seed: int = 0, part: int = 0) -> dict:
    streams_of = jax.random.split(jax.random.key(seed), 6)
    own_keys = jax.random.split(jax.random.fold_in(streams_of[5], part), 6)
    return {
        "hyena_in": normal_values(own_keys[0], (STREAMS, LENGTH, 3, D), 1.0, 6.0, ((0, 2), (1, 4), (3, 2))),
        "short_filter": normal_values(streams_of[1], (3, SHORT, D), SHORT ** -0.5, 2.0, ((2, 2),)),
        "long_filter": normal_values(streams_of[2], (FILT, NFILT), FILT ** -0.5, 0.5, ((1, 2),)),
        "qkv": draw_qkv(jax.random.fold_in(jax.random.fold_in(streams_of[5], part), 71), part),
        "lengths": jax.vmap(lambda own: uneven(own, NSEQ, LENGTH, 3 * LENGTH // 4, 2))(jax.random.split(own_keys[4], STREAMS)).reshape((STREAMS, NSEQ)).astype(jnp.int32),
    }


def sequence_ids(lengths_row, count):
    ends = jnp.cumsum(lengths_row)[:-1].astype(jnp.int32)
    places = jnp.arange(count, dtype=jnp.int32)
    return lax.optimization_barrier(jnp.sum((places[:, None] >= ends[None, :]).astype(jnp.int32), axis=1))

def delayed(values, lag, fill):
    if lag == 0:
        return values
    padding = jnp.full((lag,) + values.shape[1:], fill, values.dtype)
    return jnp.concatenate([padding, values[:values.shape[0] - lag]], axis=0)

def hyena_stream(streams, idents, short_filter, long_filter):
    inputs = streams.astype(jnp.float32)
    mixed = jnp.zeros(inputs.shape, jnp.float32)
    for tap in range(SHORT):
        keep = (delayed(idents, tap, -1) == idents).astype(jnp.float32)
        mixed = mixed + short_filter[:, tap, :].astype(jnp.float32)[None] * delayed(inputs, tap, 0.0) * keep[:, None, None]
    rounded = lax.optimization_barrier((mixed[:, 0] * mixed[:, 2]).astype(jnp.bfloat16))
    product = rounded.astype(jnp.float32)
    taps_full = jnp.repeat(long_filter.astype(jnp.float32), GROUP, axis=1)
    conv = jnp.zeros(product.shape, jnp.float32)
    for tap in range(FILT):
        keep = (delayed(idents, tap, -1) == idents).astype(jnp.float32)
        conv = conv + taps_full[tap][None] * delayed(product, tap, 0.0) * keep[:, None]
    return (mixed[:, 1] * conv).astype(jnp.bfloat16)

def attention_stream(block, idents):
    count = block.shape[0]
    scale = 1.0 / math.sqrt(HD)
    places = jnp.arange(count, dtype=jnp.int32)
    admit = (places[:, None] >= places[None, :]) & (idents[:, None] == idents[None, :])
    slabs = block.reshape(count, 3, H, HD).transpose(2, 1, 0, 3)

    def one_head(slab):
        scores = jnp.dot(slab[0], slab[1].T, preferred_element_type=jnp.float32) * scale
        scores = jnp.where(admit, scores, -jnp.inf)
        peak = lax.optimization_barrier(jnp.max(scores, axis=1, keepdims=True))
        weights = jnp.where(admit, jnp.exp(scores - peak), 0.0)
        total = lax.optimization_barrier(jnp.sum(weights, axis=1, keepdims=True))
        mixed = jnp.dot(weights.astype(jnp.bfloat16), slab[2], preferred_element_type=jnp.float32)
        return mixed / total
    outputs = lax.map(one_head, slabs)
    return outputs.transpose(1, 0, 2).reshape(count, H * HD).astype(jnp.bfloat16)

def reference(hyena_in, short_filter, long_filter, qkv, lengths):
    mixer_parts = []
    attention_parts = []
    for stream in range(STREAMS):
        idents = sequence_ids(lengths[stream], hyena_in.shape[1])
        mixer_parts.append(hyena_stream(hyena_in[stream], idents, short_filter, long_filter))
        attention_parts.append(attention_stream(qkv[stream], idents))
    return (jnp.stack(mixer_parts, 0), jnp.stack(attention_parts, 0))
```

```python
from functools import partial
import math

import jax
import jax.numpy as jnp
from jax import lax
from jax.experimental import pallas as pl
from jax.experimental.pallas import tpu as pltpu
from jax.sharding import PartitionSpec as P

H = 64
LANES = 128
CHUNKS = 2
NEG = -1e30
FLOOR = -1e29


def bounds_of(lengths_ref):
    ends, total = [], 0
    for i in range(lengths_ref.shape[1] - 1):
        total = total + lengths_ref[0, i]
        ends.append(total)
    return ends


def start_of(places, ends):
    start = jnp.zeros(places.shape, jnp.int32)
    for end in ends:
        start = jnp.where(places >= end, end, start)
    return start


def tail_kernel(where_ref, lengths_ref, x_ref, taps_ref, out_ref, line, keep):
    count = x_ref.shape[1]
    reach = line.shape[1]
    first = count - reach
    short = taps_ref.shape[1]
    ends = bounds_of(lengths_ref)
    anchor = where_ref[0] * count

    @pl.when(pl.program_id(0) == 0)
    def _():
        place = anchor + first + lax.broadcasted_iota(jnp.int32, (reach, LANES), 0)
        start = start_of(place, ends)
        for tap in range(short):
            keep[tap] = (place - tap >= start).astype(jnp.float32)

    def one(i, carry):
        lanes = pl.ds(pl.multiple_of(i * LANES, LANES), LANES)
        mixed = []
        for which, slot in enumerate((0, 2)):
            line[which] = x_ref[slot, first:count, lanes].astype(jnp.float32)
            head = x_ref[slot, first - 16:first, lanes].astype(jnp.float32)
            total = taps_ref[slot, 0:1, lanes].astype(jnp.float32) * line[which]
            joined = jnp.concatenate([head[8:], line[which]], axis=0)
            for tap in range(1, short):
                total = total + (
                    taps_ref[slot, tap:tap + 1, lanes].astype(jnp.float32)
                    * joined[8 - tap:8 - tap + reach]
                    * keep[tap]
                )
            mixed.append(total)
        out_ref[0:reach, lanes] = (mixed[0] * mixed[1]).astype(out_ref.dtype)
        for slot in range(3):
            out_ref[reach + 16 * slot:reach + 16 * (slot + 1), lanes] = x_ref[
                slot, count - 16:count, lanes
            ]
        return carry

    lax.fori_loop(0, x_ref.shape[2] // LANES, one, 0)


def mixer_tail(index, lengths, inputs, short_filter, reach):
    slots, count, width = inputs.shape
    block = min(width, 1024)
    short = short_filter.shape[1]
    rows = reach + 16 * slots
    return pl.pallas_call(
        tail_kernel,
        out_shape=jax.ShapeDtypeStruct((rows, width), inputs.dtype),
        grid_spec=pltpu.PrefetchScalarGridSpec(
            num_scalar_prefetch=2,
            grid=(width // block,),
            in_specs=[
                pl.BlockSpec((slots, count, block), lambda i, *_: (0, 0, i)),
                pl.BlockSpec((slots, short, block), lambda i, *_: (0, 0, i)),
            ],
            out_specs=pl.BlockSpec((rows, block), lambda i, *_: (0, i)),
            scratch_shapes=[
                pltpu.VMEM((2, reach, LANES), jnp.float32),
                pltpu.VMEM((short, reach, LANES), jnp.float32),
            ],
        ),
        name="mixer_tail",
    )(index, lengths, inputs, short_filter)


def mixer_kernel(where_ref, lengths_ref, x_ref, taps_ref, base_ref, halo_ref, out_ref,
                 line, keep, band_mask, band, window):
    slots, count, width = x_ref.shape
    reach = base_ref.shape[1]
    rest = count - reach
    short = taps_ref.shape[1]
    groups = band.shape[0] // count
    share = LANES // groups
    ends = bounds_of(lengths_ref)
    anchor = where_ref[0] * count

    @pl.when(pl.program_id(0) == 0)
    def _():
        row = lax.broadcasted_iota(jnp.int32, (count, LANES), 0)
        lane = lax.broadcasted_iota(jnp.int32, (count, LANES), 1)
        place = anchor + row
        start = start_of(place, ends)
        for tap in range(short):
            keep[tap] = (place - tap >= start).astype(jnp.float32)
        under = jnp.where(row >= reach, row - reach, row)
        shift = jnp.where(row >= reach, reach, 0)
        source = anchor - reach + shift + lane
        older = (lane > under) & (source >= start)
        newer = (lane <= under) & (source + reach >= start)
        band_mask[:, 0:LANES] = older.astype(jnp.float32).astype(band_mask.dtype)
        band_mask[:, LANES:2 * LANES] = newer.astype(jnp.float32).astype(band_mask.dtype)
        window[reach + count:, :] = jnp.zeros((reach - rest, LANES), window.dtype)

    def one(i, carry):
        lanes = pl.ds(pl.multiple_of(i * LANES, LANES), LANES)
        mixed = []
        for slot in range(slots):
            before = halo_ref[reach + 16 * slot:reach + 16 * (slot + 1), lanes]
            line[slot, 0:8] = before.astype(jnp.float32)[8:]
            line[slot, 8:8 + count] = x_ref[slot, :, lanes].astype(jnp.float32)
            total = taps_ref[slot, 0:1, lanes].astype(jnp.float32) * line[slot, 8:8 + count]
            for tap in range(1, short):
                total = total + (
                    taps_ref[slot, tap:tap + 1, lanes].astype(jnp.float32)
                    * line[slot, 8 - tap:8 - tap + count]
                    * keep[tap]
                )
            mixed.append(total)
        window[0:reach, :] = halo_ref[0:reach, lanes]
        window[reach:reach + count, :] = (mixed[0] * mixed[2]).astype(window.dtype)
        for g in range(groups):
            taps = base_ref[pl.ds(i * groups + g, 1), :]
            circle = pltpu.roll(
                jnp.broadcast_to(taps, (reach, reach)), 0, 1, stride=1, stride_axis=0
            ).astype(band.dtype)
            for half in range(2):
                cols = slice(half * LANES, (half + 1) * LANES)
                band[g * reach:(g + 1) * reach, cols] = circle * band_mask[0:reach, cols]
                band[groups * reach + g * rest:groups * reach + (g + 1) * rest, cols] = (
                    circle[0:rest] * band_mask[reach:count, cols]
                )
        upper = jnp.dot(band[0:groups * reach, :], window[0:2 * reach, :],
                        preferred_element_type=jnp.float32)
        lower = jnp.dot(band[groups * reach:, :], window[reach:3 * reach, :],
                        preferred_element_type=jnp.float32)
        owner = lax.broadcasted_iota(jnp.int32, (1, LANES), 1) // share
        top, bottom = upper[0:reach], lower[0:rest]
        for g in range(1, groups):
            top = jnp.where(owner == g, upper[g * reach:(g + 1) * reach], top)
            bottom = jnp.where(owner == g, lower[g * rest:(g + 1) * rest], bottom)
        out_ref[0:reach, lanes] = (mixed[1][0:reach] * top).astype(out_ref.dtype)
        out_ref[reach:count, lanes] = (mixed[1][reach:count] * bottom).astype(out_ref.dtype)
        return carry

    lax.fori_loop(0, width // LANES, one, 0)


def mixer(index, lengths, inputs, short_filter, base, halo):
    slots, count, width = inputs.shape
    filters, reach = base.shape
    block = min(width, 512)
    short = short_filter.shape[1]
    groups = LANES * filters // width
    rows = halo.shape[0]
    return pl.pallas_call(
        mixer_kernel,
        out_shape=jax.ShapeDtypeStruct((count, width), inputs.dtype),
        grid_spec=pltpu.PrefetchScalarGridSpec(
            num_scalar_prefetch=2,
            grid=(width // block,),
            in_specs=[
                pl.BlockSpec((slots, count, block), lambda i, *_: (0, 0, i)),
                pl.BlockSpec((slots, short, block), lambda i, *_: (0, 0, i)),
                pl.BlockSpec((filters * block // width, reach), lambda i, *_: (i, 0)),
                pl.BlockSpec((rows, block), lambda i, *_: (0, i)),
            ],
            out_specs=pl.BlockSpec((count, block), lambda i, *_: (0, i)),
            scratch_shapes=[
                pltpu.VMEM((slots, 8 + count, LANES), jnp.float32),
                pltpu.VMEM((short, count, LANES), jnp.float32),
                pltpu.VMEM((count, 2 * LANES), inputs.dtype),
                pltpu.VMEM((groups * count, 2 * LANES), inputs.dtype),
                pltpu.VMEM((3 * reach, LANES), inputs.dtype),
            ],
        ),
        name="mixer",
    )(index, lengths, inputs, short_filter, base, halo)


def parts_of(value):
    high = value.astype(jnp.bfloat16)
    rest = value - high.astype(jnp.float32)
    middle = rest.astype(jnp.bfloat16)
    low = (rest - middle.astype(jnp.float32)).astype(jnp.bfloat16)
    return high, middle, low


def attend_kernel(where_ref, lengths_ref, own_ref, near_ref, far_ref, prior_ref,
                  out_ref, out_norm_ref, near_out_ref, far_out_ref,
                  bias, norms):
    count = own_ref.shape[1]
    depth = own_ref.shape[2]
    scale = 1.0 / math.sqrt(depth)
    step = pl.program_id(0)
    last = pl.num_programs(0) - 1
    index = where_ref[0]
    ends = bounds_of(lengths_ref)
    pivot = index == 1
    helps = (index == 1) | (index == 2)

    @pl.when(step == 0)
    def _():
        row = lax.broadcasted_iota(jnp.int32, (count, 2 * count), 0)
        col = lax.broadcasted_iota(jnp.int32, (count, 2 * count), 1)
        source = (index - 1) * count + col
        held = pivot | (col >= count)
        for which in range(3):
            place = (index + which) * count + row
            ok = (source <= place) & (source >= start_of(place, ends)) & held
            bias[which] = jnp.where(ok, 0.0, NEG)
        norms[...] = jnp.zeros(norms.shape, jnp.float32)

    def head(which, queries):
        keys = jnp.concatenate([prior_ref[0], own_ref[1]], axis=0)
        values = jnp.concatenate([prior_ref[1], own_ref[2]], axis=0)
        scores = lax.dot_general(queries, keys, (((1,), (1,)), ((), ())),
                                 preferred_element_type=jnp.float32)
        scores = scores * scale + bias[which]
        peak = jnp.maximum(jnp.max(scores, axis=1, keepdims=True), FLOOR)
        weights = jnp.exp(scores - peak)
        total = jnp.sum(weights, axis=1, keepdims=True)
        mixed = jnp.dot(weights.astype(jnp.bfloat16), values, preferred_element_type=jnp.float32)
        some = total > 0.0
        safe = jnp.where(some, total, 1.0)
        norm = jnp.where(some, peak + jnp.log(safe), NEG)
        lane = lax.broadcasted_iota(jnp.int32, (count, LANES), 1)
        norms[which] = jnp.where(lane == step, norm, norms[which])
        return mixed / safe

    @pl.when(step < last)
    def _():
        out_ref[...] = head(0, own_ref[0])

        @pl.when(helps)
        def _():
            near_out_ref[...] = head(1, near_ref[...]).astype(near_out_ref.dtype)

        @pl.when(pivot)
        def _():
            far_out_ref[...] = head(2, far_ref[...]).astype(far_out_ref.dtype)

    @pl.when(step == last)
    def _():
        out_norm_ref[...] = norms[0]
        for which, ref in ((1, near_out_ref), (2, far_out_ref)):
            high, middle, low = parts_of(norms[which])
            spread = LANES // 4
            total = high.astype(jnp.float32)
            total = total + pltpu.roll(middle.astype(jnp.float32), spread, 1)
            total = total + pltpu.roll(low.astype(jnp.float32), 2 * spread, 1)
            ref[...] = total.astype(ref.dtype)


def attend_part(index, lengths, blocks, near, far, prior, first):
    slots, count, _ = blocks.shape
    width = near.shape[1]
    heads = width // LANES
    clamp = lambda i: jnp.minimum(i, heads - 1)
    return pl.pallas_call(
        attend_kernel,
        out_shape=(
            jax.ShapeDtypeStruct((count, width), jnp.float32),
            jax.ShapeDtypeStruct((count, LANES), jnp.float32),
            jax.ShapeDtypeStruct((count, width + LANES), near.dtype),
            jax.ShapeDtypeStruct((count, width + LANES), near.dtype),
        ),
        grid_spec=pltpu.PrefetchScalarGridSpec(
            num_scalar_prefetch=2,
            grid=(heads + 1,),
            in_specs=[
                pl.BlockSpec((slots, count, LANES), lambda i, *_: (0, 0, first + clamp(i))),
                pl.BlockSpec((count, LANES), lambda i, *_: (0, clamp(i))),
                pl.BlockSpec((count, LANES), lambda i, *_: (0, clamp(i))),
                pl.BlockSpec((2, count, LANES), lambda i, *_: (0, 0, clamp(i))),
            ],
            out_specs=(
                pl.BlockSpec((count, LANES), lambda i, *_: (0, clamp(i))),
                pl.BlockSpec((count, LANES), lambda i, *_: (0, 0)),
                pl.BlockSpec((count, LANES), lambda i, *_: (0, i)),
                pl.BlockSpec((count, LANES), lambda i, *_: (0, i)),
            ),
            scratch_shapes=[
                pltpu.VMEM((3, count, 2 * count), jnp.float32),
                pltpu.VMEM((3, count, LANES), jnp.float32),
            ],
        ),
        name="attend_part",
    )(index, lengths, blocks, near, far, prior)


def merge_kernel(where_ref, own_ref, own_norm_ref, near_ref, far_ref, out_ref):
    count, width = own_ref.shape
    heads = width // LANES
    index = where_ref[0]
    spread = LANES // 4

    def norm_of(ref, used):
        packed = ref[:, width:width + LANES].astype(jnp.float32)
        total = packed + pltpu.roll(packed, LANES - spread, 1)
        total = total + pltpu.roll(packed, LANES - 2 * spread, 1)
        return jnp.where(used, total, NEG)

    @pl.when(index < 2)
    def _():
        out_ref[...] = own_ref[...].astype(out_ref.dtype)

    @pl.when(index >= 2)
    def _():
        own = own_norm_ref[...]
        near = norm_of(near_ref, index >= 2)
        far = norm_of(far_ref, index == 3)
        peak = jnp.maximum(own, jnp.maximum(near, far))
        own_part = jnp.exp(own - peak)
        near_part = jnp.exp(near - peak)
        far_part = jnp.exp(far - peak)
        whole = own_part + near_part + far_part
        own_part, near_part, far_part = own_part / whole, near_part / whole, far_part / whole
        for h in range(heads):
            lanes = slice(h * LANES, (h + 1) * LANES)
            mixed = own_ref[:, lanes] * own_part[:, h:h + 1]
            mixed = mixed + near_ref[:, lanes].astype(jnp.float32) * near_part[:, h:h + 1]
            mixed = mixed + jnp.where(
                index == 3, far_ref[:, lanes].astype(jnp.float32) * far_part[:, h:h + 1], 0.0
            )
            out_ref[:, lanes] = mixed.astype(out_ref.dtype)


def merge_part(index, own, own_norm, near, far):
    count, width = own.shape
    return pl.pallas_call(
        merge_kernel,
        out_shape=jax.ShapeDtypeStruct((count, width), near.dtype),
        grid_spec=pltpu.PrefetchScalarGridSpec(
            num_scalar_prefetch=1,
            grid=(1,),
            in_specs=[
                pl.BlockSpec((count, width), lambda i, *_: (0, 0)),
                pl.BlockSpec((count, LANES), lambda i, *_: (0, 0)),
                pl.BlockSpec((count, width + LANES), lambda i, *_: (0, 0)),
                pl.BlockSpec((count, width + LANES), lambda i, *_: (0, 0)),
            ],
            out_specs=pl.BlockSpec((count, width), lambda i, *_: (0, 0)),
        ),
        name="merge_part",
    )(index, own, own_norm, near, far)


def attend_four(index, lengths, blocks):
    slots, count, width = blocks.shape
    part = width // CHUNKS
    outs = []
    for c in range(CHUNKS):
        cols = slice(c * part, (c + 1) * part)
        prior = lax.ppermute(blocks[1:3, :, cols], "ctx", [(0, 1)])
        near = lax.ppermute(blocks[0, :, cols], "ctx", [(2, 1), (3, 2)])
        far = lax.ppermute(blocks[0, :, cols], "ctx", [(3, 1)])
        own, own_norm, near_out, far_out = attend_part(
            index, lengths, blocks, near, far, prior, c * part // LANES
        )
        near_in = lax.ppermute(near_out, "ctx", [(1, 2), (2, 3)])
        far_in = lax.ppermute(far_out, "ctx", [(1, 3)])
        outs.append(merge_part(index, own, own_norm, near_in, far_in))
    return jnp.concatenate(outs, axis=1)


def attend_any(lengths, blocks, heads):
    count, width = blocks.shape[1:]
    depth = width // heads
    bounds = jnp.cumsum(lengths[0])[:-1]
    gathered = lax.all_gather(blocks[1:3], "ctx", axis=1, tiled=True)
    extent = gathered.shape[1]
    place = lax.axis_index("ctx") * count + jnp.arange(count, dtype=jnp.int32)
    source = jnp.arange(extent, dtype=jnp.int32)
    start = jnp.max(jnp.where(place[:, None] >= bounds[None, :], bounds[None, :], 0), axis=1)
    admit = (source[None, :] <= place[:, None]) & (source[None, :] >= start[:, None])
    queries = blocks[0].reshape(count, heads, depth)
    keys = gathered[0].reshape(extent, heads, depth)
    values = gathered[1].reshape(extent, heads, depth)
    scores = jnp.einsum("thd,shd->hts", queries, keys, preferred_element_type=jnp.float32)
    scores = jnp.where(admit[None], scores * (1.0 / math.sqrt(depth)), NEG)
    peak = jnp.max(scores, axis=2, keepdims=True)
    weights = jnp.where(admit[None], jnp.exp(scores - peak), 0.0)
    total = jnp.sum(weights, axis=2)
    mixed = jnp.einsum("hts,shd->htd", weights.astype(jnp.bfloat16), values,
                       preferred_element_type=jnp.float32)
    mixed = mixed / total[:, :, None]
    return mixed.transpose(1, 0, 2).reshape(count, width).astype(jnp.bfloat16)


def on_device(hyena_in, short_filter, long_filter, qkv, lengths):
    size = lax.axis_size("ctx")
    index = lax.axis_index("ctx").astype(jnp.int32).reshape(1)
    inputs = hyena_in[0].transpose(1, 0, 2)
    blocks = qkv[0].transpose(1, 0, 2)
    reach = long_filter.shape[0]
    taps = long_filter.astype(jnp.float32).T
    base = jnp.concatenate([taps[:, :1], taps[:, :0:-1]], axis=1)
    tail = mixer_tail(index, lengths, inputs, short_filter, reach)
    halo = lax.ppermute(tail, "ctx", [(i, i + 1) for i in range(size - 1)])
    hyena_out = mixer(index, lengths, inputs, short_filter, base, halo)
    heads = H // lax.axis_size("tp")
    if size == 4:
        attn_out = attend_four(index, lengths, blocks)
    else:
        attn_out = attend_any(lengths, blocks, heads)
    return (hyena_out[None], attn_out[None])


def solution(mesh):
    in_specs = (
        P(("groups", "dp"), "ctx", None, "tp"),
        P(None, None, "tp"),
        P(None, "tp"),
        P(("groups", "dp"), "ctx", None, "tp"),
        P(("groups", "dp"), None),
    )
    out_specs = (P(("groups", "dp"), "ctx", "tp"), P(("groups", "dp"), "ctx", "tp"))
    return jax.shard_map(
        on_device, mesh=mesh, in_specs=in_specs, out_specs=out_specs, check_vma=False
    )
```

```python
from functools import partial
import math

import jax
import jax.numpy as jnp
from jax import lax
from jax.experimental import pallas as pl
from jax.experimental.pallas import tpu as pltpu
from jax.sharding import PartitionSpec as P

H = 64
LANES = 128
ROWS = 32
TAIL_BLOCK = 1024
MIX_BLOCK = 512
HEADS_AT_ONCE = 4
CHUNKS = 2
SPREAD = LANES // 6
NEG = -1e30
FLOOR = -1e29


def bounds_of(lengths_ref):
    ends, total = [], 0
    for i in range(lengths_ref.shape[1] - 1):
        total = total + lengths_ref[0, i]
        ends.append(total)
    return ends


def start_of(places, ends):
    start = jnp.zeros(places.shape, jnp.int32)
    for end in ends:
        start = jnp.where(places >= end, end, start)
    return start


def filtered(line, offset, taps, keep, first, rows):
    outs = []
    for part in range(line.shape[0]):
        lanes = slice(part * LANES, (part + 1) * LANES)
        total = taps[0:1, lanes] * line[part, offset + first:offset + first + rows]
        for tap in range(1, keep.shape[0]):
            at = offset + first - tap
            total = total + taps[tap:tap + 1, lanes] * (
                line[part, at:at + rows] * keep[tap, first:first + rows]
            )
        outs.append(total)
    return jnp.concatenate(outs, axis=1)


def keep_taps(keep, anchor, ends):
    short, count, _ = keep.shape
    place = anchor + lax.broadcasted_iota(jnp.int32, (count, LANES), 0)
    start = start_of(place, ends)
    for tap in range(short):
        keep[tap] = (place - tap >= start).astype(jnp.float32)


def tail_kernel(where_ref, lengths_ref, gate_ref, value_ref, last_ref, taps_ref, *refs):
    *refs, line, keep, taps = refs
    extra = len(refs) // 2
    slab_refs, out_ref, message_refs = refs[:extra], refs[extra], refs[extra + 1:]
    count, width = gate_ref.shape
    reach = out_ref.shape[0] - 32
    first = count - reach
    short = taps_ref.shape[1]
    parts = line.shape[1]
    wide = parts * LANES

    @pl.when(pl.program_id(0) == 0)
    def _():
        keep_taps(keep, where_ref[0] * count, bounds_of(lengths_ref))

    taps[:, 0:short] = taps_ref[...].astype(jnp.float32)
    ends = [ref[ref.shape[0] - 16:].astype(jnp.float32)[8:] for ref in (gate_ref, last_ref, value_ref)]
    ends = jnp.concatenate(ends + [jnp.zeros((8, width), jnp.float32)], axis=0)
    out_ref[reach:reach + 32] = ends.astype(out_ref.dtype)

    def one(i, carry):
        lanes = pl.ds(pl.multiple_of(i * wide, LANES), wide)
        for which, ref in enumerate((gate_ref, value_ref)):
            for part in range(parts):
                here = pl.ds(pl.multiple_of(i * wide + part * LANES, LANES), LANES)
                line[which, part] = ref[:, here].astype(jnp.float32)
        for at in range(first, count, ROWS):
            gate = filtered(line.at[0], 0, taps[0, :, lanes], keep, at, ROWS)
            value = filtered(line.at[1], 0, taps[2, :, lanes], keep, at, ROWS)
            out_ref[at - first:at - first + ROWS, lanes] = (gate * value).astype(out_ref.dtype)
        return carry

    lax.fori_loop(0, width // wide, one, 0)

    for slab_ref, message_ref in zip(slab_refs, message_refs):
        @pl.when(where_ref[0] == 0)
        def _():
            message_ref[0:count] = slab_ref[...]
            message_ref[count:] = jnp.zeros((reach + 32 - count, width), message_ref.dtype)

        @pl.when(where_ref[0] != 0)
        def _():
            message_ref[...] = out_ref[...]


def mixer_tail(index, lengths, inputs, short_filter, reach, first, cols, blocks=None, slab=0):
    slots, count, _ = inputs.shape
    block = min(cols, 1024)
    short = short_filter.shape[1]
    rows = reach + 32
    start = first // block
    out = jax.ShapeDtypeStruct((rows, cols), inputs.dtype)
    out_spec = pl.BlockSpec((rows, block), lambda i, *_: (0, i))
    extra = () if blocks is None else (blocks,)
    return pl.pallas_call(
        tail_kernel,
        out_shape=(out,) * (1 + len(extra)),
        grid_spec=pltpu.PrefetchScalarGridSpec(
            num_scalar_prefetch=2,
            grid=(cols // block,),
            in_specs=[
                pl.BlockSpec((None, count, block), lambda i, *_: (0, 0, start + i)),
                pl.BlockSpec((None, count, block), lambda i, *_: (2, 0, start + i)),
                pl.BlockSpec((None, 16, block), lambda i, *_: (1, count // 16 - 1, start + i)),
                pl.BlockSpec((slots, short, block), lambda i, *_: (0, 0, start + i)),
            ]
            + [pl.BlockSpec((None, count, block), lambda i, *_: (1 + i, 0, slab))] * len(extra),
            out_specs=(out_spec,) * (1 + len(extra)),
            scratch_shapes=[
                pltpu.VMEM((2, 2, count, LANES), jnp.float32),
                pltpu.VMEM((short, count, LANES), jnp.float32),
                pltpu.VMEM((slots, 8, block), jnp.float32),
            ],
        ),
        name="mixer_tail",
    )(index, lengths, inputs, inputs, inputs, short_filter, *extra)


def mixer_kernel(where_ref, lengths_ref, x1_ref, x2_ref, v_ref, taps_ref, base_ref, tail_ref, *refs):
    *halo_refs, out_ref, line, keep, taps, band_mask, band, window, gate = refs
    halo_refs = [ref for ref in halo_refs if ref.shape == tail_ref.shape]
    slots = taps_ref.shape[0]
    count, width = x2_ref.shape
    reach = base_ref.shape[1]
    rest = count - reach
    short = taps_ref.shape[1]
    parts = line.shape[1]
    wide = parts * LANES
    groups = band.shape[1] // count
    share = LANES // groups
    ends = bounds_of(lengths_ref)
    anchor = where_ref[0] * count

    @pl.when(pl.program_id(0) == 0)
    def _():
        keep_taps(keep, anchor, ends)
        row = lax.broadcasted_iota(jnp.int32, (count, LANES), 0)
        lane = lax.broadcasted_iota(jnp.int32, (count, LANES), 1)
        start = start_of(anchor + row, ends)
        under = jnp.where(row >= reach, row - reach, row)
        shift = jnp.where(row >= reach, reach, 0)
        source = anchor - reach + shift + lane
        older = (lane > under) & (source >= start)
        newer = (lane <= under) & (source + reach >= start)
        band_mask[:, 0:LANES] = older.astype(jnp.float32).astype(band_mask.dtype)
        band_mask[:, LANES:2 * LANES] = newer.astype(jnp.float32).astype(band_mask.dtype)
        window[reach + count:, :] = jnp.zeros((reach - rest, wide), window.dtype)

    taps[:, 0:short] = taps_ref[...].astype(jnp.float32)
    owner = lax.broadcasted_iota(jnp.int32, (1, LANES), 1) // share

    def halo(rows, lanes):
        total = halo_refs[0][rows, lanes]
        for ref in halo_refs[1:]:
            total = jnp.where(where_ref[0] == 1, ref[rows, lanes], total)
        return total

    def one(i, carry):
        lanes = pl.ds(pl.multiple_of(i * wide, LANES), wide)
        for part in range(parts):
            here = pl.ds(pl.multiple_of(i * wide + part * LANES, LANES), LANES)
            for slot, ref in enumerate((x1_ref, x2_ref, v_ref)):
                line[slot, part, 8:16] = halo(slice(reach, reach + 32), here).astype(jnp.float32)[
                    8 * slot:8 * slot + 8
                ]
                line[slot, part, 16:16 + ref.shape[0]] = ref[:, here].astype(jnp.float32)
        first = [filtered(line.at[slot], 16, taps[slot, :, lanes], keep, 0, rest) for slot in (0, 2)]
        window[0:reach] = halo(slice(0, reach), lanes)
        window[reach:reach + rest] = (first[0] * first[1]).astype(window.dtype)
        window[reach + rest:reach + count] = tail_ref[0:reach, lanes]
        for at in range(0, count, 48):
            gate[at:at + 48] = filtered(line.at[1], 16, taps[1, :, lanes], keep, at, 48)
        for part in range(wide // LANES):
            held = band.at[part]
            for g in range(groups):
                row = base_ref[pl.ds((i * (wide // LANES) + part) * groups + g, 1), :]
                circle = pltpu.roll(
                    jnp.broadcast_to(row, (reach, reach)), 0, 1, stride=1, stride_axis=0
                ).astype(band.dtype)
                for half in range(2):
                    cols = slice(half * LANES, (half + 1) * LANES)
                    held[g * reach:(g + 1) * reach, cols] = circle * band_mask[0:reach, cols]
                    held[groups * reach + g * rest:groups * reach + (g + 1) * rest, cols] = (
                        circle[0:rest] * band_mask[reach:count, cols]
                    )
            here = slice(part * LANES, (part + 1) * LANES)
            upper = jnp.dot(held[0:groups * reach, :], window[0:2 * reach, here],
                            preferred_element_type=jnp.float32)
            lower = jnp.dot(held[groups * reach:, :], window[reach:3 * reach, here],
                            preferred_element_type=jnp.float32)
            top, bottom = upper[0:reach], lower[0:rest]
            for g in range(1, groups):
                top = jnp.where(owner == g, upper[g * reach:(g + 1) * reach], top)
                bottom = jnp.where(owner == g, lower[g * rest:(g + 1) * rest], bottom)
            out_lanes = pl.ds(pl.multiple_of(i * wide + part * LANES, LANES), LANES)
            out_ref[0:reach, out_lanes] = (gate[0:reach, here] * top).astype(out_ref.dtype)
            out_ref[reach:count, out_lanes] = (gate[reach:count, here] * bottom).astype(out_ref.dtype)
        return carry

    lax.fori_loop(0, width // wide, one, 0)


def mixer(index, lengths, inputs, short_filter, base, tail, halos, first=0, held=None):
    slots, count, width = inputs.shape
    filters, reach = base.shape
    rows, cols = tail.shape
    block = min(cols, 512)
    short = short_filter.shape[1]
    groups = LANES * filters // width
    wide = 2 * LANES
    start = first // block
    extra = () if held is None else (held,)
    operands = (index, lengths, inputs, inputs, inputs, short_filter, base, tail, *halos, *extra)
    return pl.pallas_call(
        mixer_kernel,
        out_shape=jax.ShapeDtypeStruct((count, width), inputs.dtype),
        grid_spec=pltpu.PrefetchScalarGridSpec(
            num_scalar_prefetch=2,
            grid=(cols // block,),
            in_specs=[
                pl.BlockSpec((None, count - reach, block), lambda i, *_: (0, 0, start + i)),
                pl.BlockSpec((None, count, block), lambda i, *_: (1, 0, start + i)),
                pl.BlockSpec((None, count - reach, block), lambda i, *_: (2, 0, start + i)),
                pl.BlockSpec((slots, short, block), lambda i, *_: (0, 0, start + i)),
                pl.BlockSpec((filters * block // width, reach), lambda i, *_: (start + i, 0)),
                pl.BlockSpec((rows, block), lambda i, *_: (0, i)),
            ]
            + [pl.BlockSpec((rows, block), lambda i, *_: (0, i))] * len(halos)
            + [pl.BlockSpec(memory_space=pl.ANY)] * len(extra),
            out_specs=pl.BlockSpec((count, block), lambda i, *_: (0, start + i)),
            scratch_shapes=[
                pltpu.VMEM((slots, wide // LANES, 16 + count, LANES), jnp.float32),
                pltpu.VMEM((short, count, LANES), jnp.float32),
                pltpu.VMEM((slots, 8, block), jnp.float32),
                pltpu.VMEM((count, 2 * LANES), inputs.dtype),
                pltpu.VMEM((wide // LANES, groups * count, 2 * LANES), inputs.dtype),
                pltpu.VMEM((3 * reach, wide), inputs.dtype),
                pltpu.VMEM((count, wide), jnp.float32),
            ],
        ),
        input_output_aliases={len(operands) - 1: 0} if extra else {},
        name="mixer",
    )(*operands)


def parts_of(value):
    high = value.astype(jnp.bfloat16)
    rest = value - high.astype(jnp.float32)
    middle = rest.astype(jnp.bfloat16)
    low = (rest - middle.astype(jnp.float32)).astype(jnp.bfloat16)
    return high, middle, low


def attend_kernel(where_ref, lengths_ref, own_ref, near_ref, far_ref, prior_ref,
                  out_ref, out_peak_ref, out_total_ref, near_out_ref, far_out_ref, bias, peaks, totals):
    count = own_ref.shape[1]
    width = near_ref.shape[1]
    heads = width // LANES
    scale = 1.0 / math.sqrt(LANES)
    index = where_ref[0]
    ends = bounds_of(lengths_ref)
    pivot = index == 1

    def mask(groups, keys, first):
        row = lax.broadcasted_iota(jnp.int32, (count, keys), 0)
        source = first + lax.broadcasted_iota(jnp.int32, (count, keys), 1)
        for which in range(groups):
            place = (index + which) * count + row
            ok = (source <= place) & (source >= start_of(place, ends))
            bias[which * count:(which + 1) * count, 0:keys] = jnp.where(ok, 0.0, NEG)

    rate = scale * math.log2(math.e)

    def softmax(queries, keys, values):
        rows, extent = queries.shape[0], keys.shape[0]
        scores = lax.dot_general(queries, keys, (((1,), (1,)), ((), ())),
                                 preferred_element_type=jnp.float32)
        scores = scores + bias[0:rows, 0:extent]
        peak = jnp.maximum(jnp.max(scores, axis=1, keepdims=True), FLOOR)
        weights = jnp.exp2((scores - peak) * rate).astype(jnp.bfloat16)
        wide = jnp.concatenate([values, jnp.ones(values.shape, values.dtype)], axis=1)
        mixed = jnp.dot(weights, wide, preferred_element_type=jnp.float32)
        return mixed[:, :LANES], peak, mixed[:, LANES:]

    lane = lax.broadcasted_iota(jnp.int32, (1, LANES), 1)

    def several(one, rows):
        peaks[0:rows] = jnp.zeros((rows, LANES), jnp.float32)
        totals[0:rows] = jnp.zeros((rows, LANES), jnp.float32)
        def body(i, carry):
            peak_of, total_of = peaks[0:rows], totals[0:rows]
            for u in range(HEADS_AT_ONCE):
                h = i * HEADS_AT_ONCE + u
                peak, total = one(h)
                peak_of = jnp.where(lane == h, peak, peak_of)
                total_of = jnp.where(lane == h, total, total_of)
            peaks[0:rows], totals[0:rows] = peak_of, total_of
            return carry
        lax.fori_loop(0, heads // HEADS_AT_ONCE, body, 0)

    @pl.when(pivot)
    def _():
        mask(3, 2 * count, (index - 1) * count)
        def one(h):
            lanes = pl.ds(pl.multiple_of(h * LANES, LANES), LANES)
            queries = jnp.concatenate([own_ref[0, :, lanes], near_ref[:, lanes], far_ref[:, lanes]], axis=0)
            if len(prior_ref.shape) == 3:
                before = prior_ref[0, :, lanes], prior_ref[1, :, lanes]
            else:
                beside = pl.ds(pl.multiple_of(width + h * LANES, LANES), LANES)
                before = prior_ref[0:count, lanes], prior_ref[0:count, beside]
            keys = jnp.concatenate([before[0], own_ref[1, :, lanes]], axis=0)
            values = jnp.concatenate([before[1], own_ref[2, :, lanes]], axis=0)
            mixed, peak, total = softmax(queries, keys, values)
            out_ref[:, lanes] = mixed[0:count]
            near_out_ref[:, lanes] = mixed[count:2 * count].astype(near_out_ref.dtype)
            far_out_ref[:, lanes] = mixed[2 * count:].astype(far_out_ref.dtype)
            return peak, total
        several(one, 3 * count)

    @pl.when(jnp.logical_not(pivot))
    def _():
        mask(2, count, index * count)
        def one(h):
            lanes = pl.ds(pl.multiple_of(h * LANES, LANES), LANES)
            queries = jnp.concatenate([own_ref[0, :, lanes], near_ref[:, lanes]], axis=0)
            mixed, peak, total = softmax(queries, own_ref[1, :, lanes], own_ref[2, :, lanes])
            out_ref[:, lanes] = mixed[0:count]
            near_out_ref[:, lanes] = mixed[count:].astype(near_out_ref.dtype)
            return peak, total
        several(one, 2 * count)

    out_peak_ref[...] = peaks[0:count]
    out_total_ref[...] = totals[0:count]
    for which, ref in ((1, near_out_ref), (2, far_out_ref)):
        rows = slice(which * count, (which + 1) * count)
        packed = jnp.zeros((count, LANES), jnp.float32)
        for at, piece in enumerate(parts_of(peaks[rows]) + parts_of(totals[rows])):
            piece = piece.astype(jnp.float32)
            packed = packed + (pltpu.roll(piece, at * SPREAD, 1) if at else piece)
        ref[:, width:width + LANES] = packed.astype(ref.dtype)

def attend_part(index, lengths, blocks, near, far, prior, first, width, at):
    slots, count, _ = blocks.shape
    whole = lambda i, *_: (0, 0)
    return pl.pallas_call(
        attend_kernel,
        out_shape=(
            jax.ShapeDtypeStruct((count, width), jnp.float32),
            jax.ShapeDtypeStruct((count, LANES), jnp.float32),
            jax.ShapeDtypeStruct((count, LANES), jnp.float32),
            jax.ShapeDtypeStruct((count, width + LANES), near.dtype),
            jax.ShapeDtypeStruct((count, width + LANES), near.dtype),
        ),
        grid_spec=pltpu.PrefetchScalarGridSpec(
            num_scalar_prefetch=2,
            grid=(1,),
            in_specs=[
                pl.BlockSpec((slots, count, width), lambda i, *_: (0, 0, first)),
                pl.BlockSpec((count, width), lambda i, *_: (0, at)),
                pl.BlockSpec((count, width), lambda i, *_: (0, at)),
                pl.BlockSpec(prior.shape, lambda i, *_: (0,) * prior.ndim),
            ],
            out_specs=(
                pl.BlockSpec((count, width), whole),
                pl.BlockSpec((count, LANES), whole),
                pl.BlockSpec((count, LANES), whole),
                pl.BlockSpec((count, width + LANES), whole),
                pl.BlockSpec((count, width + LANES), whole),
            ),
            scratch_shapes=[
                pltpu.VMEM((3 * count, 2 * count), jnp.float32),
                pltpu.VMEM((3 * count, LANES), jnp.float32),
                pltpu.VMEM((3 * count, LANES), jnp.float32),
            ],
        ),
        compiler_params=pltpu.CompilerParams(vmem_limit_bytes=48 << 20),
        name="attend_part",
    )(index, lengths, blocks, near, far, prior)

def merge_kernel(where_ref, own_ref, own_peak_ref, own_total_ref, near_ref, far_ref, *refs):
    out_ref = refs[-1]
    count, width = own_ref.shape
    index = where_ref[0]
    rate = math.log2(math.e) / math.sqrt(LANES)

    def stats(ref):
        packed = ref[:, width:width + LANES].astype(jnp.float32)
        pieces = [packed] + [pltpu.roll(packed, LANES - at * SPREAD, 1) for at in range(1, 6)]
        return pieces[0] + pieces[1] + pieces[2], pieces[3] + pieces[4] + pieces[5]

    @pl.when(index < 2)
    def _():
        part = 1.0 / jnp.where(own_total_ref[...] > 0.0, own_total_ref[...], 1.0)
        for h in range(width // LANES):
            lanes = slice(h * LANES, (h + 1) * LANES)
            out_ref[:, lanes] = (own_ref[:, lanes] * part[:, h:h + 1]).astype(out_ref.dtype)

    @pl.when(index >= 2)
    def _():
        both = index == 3
        own, total = own_peak_ref[...], own_total_ref[...]
        near, near_total = stats(near_ref)
        far, far_total = stats(far_ref)
        far = jnp.where(both, far, NEG)
        peak = jnp.maximum(own, jnp.maximum(near, far))
        own_part = jnp.exp2((own - peak) * rate)
        near_part = jnp.exp2((near - peak) * rate)
        far_part = jnp.exp2((far - peak) * rate)
        whole = own_part * total + near_part * near_total
        whole = whole + jnp.where(both, far_part * far_total, 0.0)
        whole = 1.0 / jnp.where(whole > 0.0, whole, 1.0)
        own_part, near_part, far_part = own_part * whole, near_part * whole, far_part * whole
        for h in range(width // LANES):
            lanes = slice(h * LANES, (h + 1) * LANES)
            mixed = own_ref[:, lanes] * own_part[:, h:h + 1]
            mixed = mixed + near_ref[:, lanes].astype(jnp.float32) * near_part[:, h:h + 1]
            mixed = mixed + jnp.where(
                both, far_ref[:, lanes].astype(jnp.float32) * far_part[:, h:h + 1], 0.0
            )
            out_ref[:, lanes] = mixed.astype(out_ref.dtype)


def merge_part(index, own, own_peak, own_total, near, far, first, full, held):
    count, width = own.shape
    whole = lambda i, *_: (0, 0)
    extra = () if held is None else (held,)
    return pl.pallas_call(
        merge_kernel,
        out_shape=jax.ShapeDtypeStruct((count, full), near.dtype),
        grid_spec=pltpu.PrefetchScalarGridSpec(
            num_scalar_prefetch=1,
            grid=(1,),
            in_specs=[
                pl.BlockSpec((count, width), whole),
                pl.BlockSpec((count, LANES), whole),
                pl.BlockSpec((count, LANES), whole),
                pl.BlockSpec((count, width + LANES), whole),
                pl.BlockSpec((count, width + LANES), whole),
            ]
            + [pl.BlockSpec(memory_space=pl.ANY)] * len(extra),
            out_specs=pl.BlockSpec((count, width), lambda i, *_: (0, first)),
        ),
        input_output_aliases={6: 0} if extra else {},
        name="merge_part",
    )(index, own, own_peak, own_total, near, far, *extra)


def layer_four(index, lengths, inputs, short_filter, base, blocks):
    reach = base.shape[1]
    width = blocks.shape[2]
    part = width // CHUNKS
    after = lax.optimization_barrier
    moved = []
    for c in range(CHUNKS):
        cols = slice(c * part, (c + 1) * part)
        prior = lax.ppermute(blocks[1:3, :, cols], "ctx", [(0, 1)])
        near = lax.ppermute(blocks[0, :, cols], "ctx", [(2, 1), (3, 2)])
        far = lax.ppermute(blocks[0, :, cols], "ctx", [(3, 1)])
        moved.append((near, far, prior))
    (tail,) = mixer_tail(index, lengths, inputs, short_filter, reach, 0, width)
    halo = lax.ppermute(tail, "ctx", [(0, 1), (1, 2), (2, 3)])
    sent, last = [], None
    for c in range(CHUNKS):
        near, far, prior = moved[c]
        if c:
            near, far, prior, _ = after((near, far, prior, last))
        own, peak, total, near_out, far_out = attend_part(
            index, lengths, blocks, near, far, prior, c, part, 0
        )
        last = near_out
        near_in = lax.ppermute(near_out, "ctx", [(1, 2), (2, 3)])
        far_in = lax.ppermute(far_out, "ctx", [(1, 3)])
        sent.append((own, peak, total, near_in, far_in))
    halo, _ = after((halo, last))
    hyena_out = mixer(index, lengths, inputs, short_filter, base, tail, [halo])
    held = None
    for c in range(CHUNKS):
        if c == CHUNKS - 1:
            held, hyena_out = after((held, hyena_out))
        held = merge_part(index, *sent[c], c, width, held)
    return hyena_out, held


def attend_any(lengths, blocks, heads):
    count, width = blocks.shape[1:]
    depth = width // heads
    bounds = jnp.cumsum(lengths[0])[:-1]
    gathered = lax.all_gather(blocks[1:3], "ctx", axis=1, tiled=True)
    extent = gathered.shape[1]
    place = lax.axis_index("ctx") * count + jnp.arange(count, dtype=jnp.int32)
    source = jnp.arange(extent, dtype=jnp.int32)
    start = jnp.max(jnp.where(place[:, None] >= bounds[None, :], bounds[None, :], 0), axis=1)
    admit = (source[None, :] <= place[:, None]) & (source[None, :] >= start[:, None])
    queries = blocks[0].reshape(count, heads, depth)
    keys = gathered[0].reshape(extent, heads, depth)
    values = gathered[1].reshape(extent, heads, depth)
    scores = jnp.einsum("thd,shd->hts", queries, keys, preferred_element_type=jnp.float32)
    scores = jnp.where(admit[None], scores * (1.0 / math.sqrt(depth)), NEG)
    peak = jnp.max(scores, axis=2, keepdims=True)
    weights = jnp.where(admit[None], jnp.exp(scores - peak), 0.0)
    total = jnp.sum(weights, axis=2)
    mixed = jnp.einsum("hts,shd->htd", weights.astype(jnp.bfloat16), values,
                       preferred_element_type=jnp.float32)
    mixed = mixed / total[:, :, None]
    return mixed.transpose(1, 0, 2).reshape(count, width).astype(jnp.bfloat16)


def on_device(hyena_in, short_filter, long_filter, qkv, lengths):
    size = lax.axis_size("ctx")
    index = lax.axis_index("ctx").astype(jnp.int32).reshape(1)
    inputs = hyena_in[0].transpose(1, 0, 2)
    blocks = qkv[0].transpose(1, 0, 2)
    reach = long_filter.shape[0]
    taps = long_filter.astype(jnp.float32).T
    base = jnp.concatenate([taps[:, :1], taps[:, :0:-1]], axis=1)
    heads = H // lax.axis_size("tp")
    if size == 4:
        hyena_out, attn_out = layer_four(index, lengths, inputs, short_filter, base, blocks)
    else:
        (tail,) = mixer_tail(index, lengths, inputs, short_filter, reach, 0, inputs.shape[2])
        halo = lax.ppermute(tail, "ctx", [(i, i + 1) for i in range(size - 1)])
        hyena_out = mixer(index, lengths, inputs, short_filter, base, tail, [halo])
        attn_out = attend_any(lengths, blocks, heads)
    return (hyena_out[None], attn_out[None])


def solution(mesh):
    in_specs = (
        P(("groups", "dp"), "ctx", None, "tp"),
        P(None, None, "tp"),
        P(None, "tp"),
        P(("groups", "dp"), "ctx", None, "tp"),
        P(("groups", "dp"), None),
    )
    out_specs = (P(("groups", "dp"), "ctx", "tp"), P(("groups", "dp"), "ctx", "tp"))
    return jax.shard_map(
        on_device, mesh=mesh, in_specs=in_specs, out_specs=out_specs, check_vma=False
    )
```

```python
from functools import partial
import math

import jax
import jax.numpy as jnp
from jax import lax
from jax.experimental import pallas as pl
from jax.experimental.pallas import tpu as pltpu
from jax.sharding import PartitionSpec as P

H = 64
LANES = 128
ROWS = 32
TAIL_BLOCK = 1024
MIX_BLOCK = 512
HEADS_AT_ONCE = 8
SPREAD = LANES // 6
NEG = -1e30
FLOOR = -1e29


def bounds_of(lengths_ref):
    ends, total = [], 0
    for i in range(lengths_ref.shape[1] - 1):
        total = total + lengths_ref[0, i]
        ends.append(total)
    return ends


def start_of(places, ends):
    start = jnp.zeros(places.shape, jnp.int32)
    for end in ends:
        start = jnp.where(places >= end, end, start)
    return start


def filtered(line, offset, taps, keep, first, rows):
    outs = []
    for part in range(line.shape[0]):
        lanes = slice(part * LANES, (part + 1) * LANES)
        total = taps[0:1, lanes] * line[part, offset + first:offset + first + rows]
        for tap in range(1, keep.shape[0]):
            at = offset + first - tap
            total = total + taps[tap:tap + 1, lanes] * (
                line[part, at:at + rows] * keep[tap, first:first + rows]
            )
        outs.append(total)
    return jnp.concatenate(outs, axis=1)


def keep_taps(keep, anchor, ends):
    short, count, _ = keep.shape
    place = anchor + lax.broadcasted_iota(jnp.int32, (count, LANES), 0)
    start = start_of(place, ends)
    for tap in range(short):
        keep[tap] = (place - tap >= start).astype(jnp.float32)


def tail_kernel(where_ref, lengths_ref, gate_ref, value_ref, last_ref, taps_ref, *refs):
    *refs, line, keep, taps = refs
    extra = len(refs) // 2
    slab_refs, out_ref, message_refs = refs[:extra], refs[extra], refs[extra + 1:]
    count, width = gate_ref.shape
    reach = out_ref.shape[0] - 24
    first = count - reach
    short = taps_ref.shape[1]
    parts = line.shape[1]
    wide = parts * LANES

    @pl.when(pl.program_id(0) == 0)
    def _():
        keep_taps(keep, where_ref[0] * count, bounds_of(lengths_ref))

    taps[:, 0:short] = taps_ref[...].astype(jnp.float32)
    ends = [ref[ref.shape[0] - 16:].astype(jnp.float32)[8:] for ref in (gate_ref, last_ref, value_ref)]
    out_ref[reach:reach + 24] = jnp.concatenate(ends, axis=0).astype(out_ref.dtype)

    def one(i, carry):
        lanes = pl.ds(pl.multiple_of(i * wide, LANES), wide)
        for which, ref in enumerate((gate_ref, value_ref)):
            for part in range(parts):
                here = pl.ds(pl.multiple_of(i * wide + part * LANES, LANES), LANES)
                line[which, part] = ref[:, here].astype(jnp.float32)
        for at in range(first, count, ROWS):
            gate = filtered(line.at[0], 0, taps[0, :, lanes], keep, at, ROWS)
            value = filtered(line.at[1], 0, taps[2, :, lanes], keep, at, ROWS)
            out_ref[at - first:at - first + ROWS, lanes] = (gate * value).astype(out_ref.dtype)
        return carry

    lax.fori_loop(0, width // wide, one, 0)

    for slab_ref, message_ref in zip(slab_refs, message_refs):
        @pl.when(where_ref[0] == 0)
        def _():
            message_ref[0:count] = slab_ref[...]
            message_ref[count:] = jnp.zeros((reach + 24 - count, width), message_ref.dtype)

        @pl.when(where_ref[0] != 0)
        def _():
            message_ref[...] = out_ref[...]


def mixer_tail(index, lengths, inputs, short_filter, reach, blocks=None, slab=0):
    slots, count, width = inputs.shape
    block = min(width, 1024)
    short = short_filter.shape[1]
    rows = reach + 24
    each = width // 2 // block
    out = jax.ShapeDtypeStruct((rows, width), inputs.dtype)
    out_spec = pl.BlockSpec((rows, block), lambda i, *_: (0, i))
    extra = () if blocks is None else (blocks,)
    return pl.pallas_call(
        tail_kernel,
        out_shape=(out,) * (1 + len(extra)),
        grid_spec=pltpu.PrefetchScalarGridSpec(
            num_scalar_prefetch=2,
            grid=(width // block,),
            in_specs=[
                pl.BlockSpec((None, count, block), lambda i, *_: (0, 0, i)),
                pl.BlockSpec((None, count, block), lambda i, *_: (2, 0, i)),
                pl.BlockSpec((None, 16, block), lambda i, *_: (1, count // 16 - 1, i)),
                pl.BlockSpec((slots, short, block), lambda i, *_: (0, 0, i)),
            ]
            + [
                pl.BlockSpec(
                    (None, count, block), lambda i, *_: (1 + i // each, 0, slab * each + i % each)
                )
            ]
            * len(extra),
            out_specs=(out_spec,) * (1 + len(extra)),
            scratch_shapes=[
                pltpu.VMEM((2, 2, count, LANES), jnp.float32),
                pltpu.VMEM((short, count, LANES), jnp.float32),
                pltpu.VMEM((slots, 8, block), jnp.float32),
            ],
        ),
        name="mixer_tail",
    )(index, lengths, inputs, inputs, inputs, short_filter, *extra)


def mixer_kernel(halos, where_ref, lengths_ref, x1_ref, x2_ref, v_ref, taps_ref, base_ref, tail_ref, *refs):
    *halo_refs, out_ref, line, keep, taps, band_mask, band, window, gate = refs
    halo_refs = halo_refs[:halos]
    slots = taps_ref.shape[0]
    count, width = x2_ref.shape
    reach = base_ref.shape[1]
    rest = count - reach
    short = taps_ref.shape[1]
    parts = line.shape[1]
    wide = parts * LANES
    groups = band.shape[1] // count
    share = LANES // groups
    ends = bounds_of(lengths_ref)
    anchor = where_ref[0] * count

    @pl.when(pl.program_id(0) == 0)
    def _():
        keep_taps(keep, anchor, ends)
        row = lax.broadcasted_iota(jnp.int32, (count, LANES), 0)
        lane = lax.broadcasted_iota(jnp.int32, (count, LANES), 1)
        start = start_of(anchor + row, ends)
        under = jnp.where(row >= reach, row - reach, row)
        shift = jnp.where(row >= reach, reach, 0)
        source = anchor - reach + shift + lane
        older = (lane > under) & (source >= start)
        newer = (lane <= under) & (source + reach >= start)
        band_mask[:, 0:LANES] = older.astype(jnp.float32).astype(band_mask.dtype)
        band_mask[:, LANES:2 * LANES] = newer.astype(jnp.float32).astype(band_mask.dtype)
        window[reach + count:, :] = jnp.zeros((reach - rest, wide), window.dtype)

    taps[:, 0:short] = taps_ref[...].astype(jnp.float32)
    owner = lax.broadcasted_iota(jnp.int32, (1, LANES), 1) // share

    def halo(rows, lanes):
        total = halo_refs[0][rows, lanes]
        for ref in halo_refs[1:]:
            total = jnp.where(where_ref[0] == 1, ref[rows, lanes], total)
        return total

    def one(i, carry):
        lanes = pl.ds(pl.multiple_of(i * wide, LANES), wide)
        for part in range(parts):
            here = pl.ds(pl.multiple_of(i * wide + part * LANES, LANES), LANES)
            for slot, ref in enumerate((x1_ref, x2_ref, v_ref)):
                line[slot, part, 8:16] = halo(slice(reach, reach + 24), here).astype(jnp.float32)[
                    8 * slot:8 * slot + 8
                ]
                line[slot, part, 16:16 + ref.shape[0]] = ref[:, here].astype(jnp.float32)
        first = [filtered(line.at[slot], 16, taps[slot, :, lanes], keep, 0, rest) for slot in (0, 2)]
        window[0:reach] = halo(slice(0, reach), lanes)
        window[reach:reach + rest] = (first[0] * first[1]).astype(window.dtype)
        window[reach + rest:reach + count] = tail_ref[0:reach, lanes]
        for at in range(0, count, 48):
            gate[at:at + 48] = filtered(line.at[1], 16, taps[1, :, lanes], keep, at, 48)
        for part in range(wide // LANES):
            held = band.at[part]
            for g in range(groups):
                row = base_ref[pl.ds((i * (wide // LANES) + part) * groups + g, 1), :]
                circle = pltpu.roll(
                    jnp.broadcast_to(row, (reach, reach)), 0, 1, stride=1, stride_axis=0
                ).astype(band.dtype)
                for half in range(2):
                    cols = slice(half * LANES, (half + 1) * LANES)
                    held[g * reach:(g + 1) * reach, cols] = circle * band_mask[0:reach, cols]
                    held[groups * reach + g * rest:groups * reach + (g + 1) * rest, cols] = (
                        circle[0:rest] * band_mask[reach:count, cols]
                    )
            here = slice(part * LANES, (part + 1) * LANES)
            upper = jnp.dot(held[0:groups * reach, :], window[0:2 * reach, here],
                            preferred_element_type=jnp.float32)
            lower = jnp.dot(held[groups * reach:, :], window[reach:3 * reach, here],
                            preferred_element_type=jnp.float32)
            top, bottom = upper[0:reach], lower[0:rest]
            for g in range(1, groups):
                top = jnp.where(owner == g, upper[g * reach:(g + 1) * reach], top)
                bottom = jnp.where(owner == g, lower[g * rest:(g + 1) * rest], bottom)
            out_lanes = pl.ds(pl.multiple_of(i * wide + part * LANES, LANES), LANES)
            out_ref[0:reach, out_lanes] = (gate[0:reach, here] * top).astype(out_ref.dtype)
            out_ref[reach:count, out_lanes] = (gate[reach:count, here] * bottom).astype(out_ref.dtype)
        return carry

    lax.fori_loop(0, width // wide, one, 0)


def mixer(index, lengths, inputs, short_filter, base, tail, halos, first, cols, held=None):
    slots, count, width = inputs.shape
    filters, reach = base.shape
    rows = tail.shape[0]
    block = min(cols, 512)
    short = short_filter.shape[1]
    groups = LANES * filters // width
    wide = 2 * LANES
    start = first // block
    extra = () if held is None else (held,)
    received = [array for array, _ in halos]
    operands = (index, lengths, inputs, inputs, inputs, short_filter, base, tail, *received, *extra)

    def columns(at):
        at = at // block
        return pl.BlockSpec((rows, block), lambda i, *_: (0, at + i))

    return pl.pallas_call(
        partial(mixer_kernel, len(halos)),
        out_shape=jax.ShapeDtypeStruct((count, width), inputs.dtype),
        grid_spec=pltpu.PrefetchScalarGridSpec(
            num_scalar_prefetch=2,
            grid=(cols // block,),
            in_specs=[
                pl.BlockSpec((None, count - reach, block), lambda i, *_: (0, 0, start + i)),
                pl.BlockSpec((None, count, block), lambda i, *_: (1, 0, start + i)),
                pl.BlockSpec((None, count - reach, block), lambda i, *_: (2, 0, start + i)),
                pl.BlockSpec((slots, short, block), lambda i, *_: (0, 0, start + i)),
                pl.BlockSpec((filters * block // width, reach), lambda i, *_: (start + i, 0)),
                columns(first),
            ]
            + [columns(at) for _, at in halos]
            + [pl.BlockSpec(memory_space=pl.ANY)] * len(extra),
            out_specs=pl.BlockSpec((count, block), lambda i, *_: (0, start + i)),
            scratch_shapes=[
                pltpu.VMEM((slots, wide // LANES, 16 + count, LANES), jnp.float32),
                pltpu.VMEM((short, count, LANES), jnp.float32),
                pltpu.VMEM((slots, 8, block), jnp.float32),
                pltpu.VMEM((count, 2 * LANES), inputs.dtype),
                pltpu.VMEM((wide // LANES, groups * count, 2 * LANES), inputs.dtype),
                pltpu.VMEM((3 * reach, wide), inputs.dtype),
                pltpu.VMEM((count, wide), jnp.float32),
            ],
        ),
        input_output_aliases={len(operands) - 1: 0} if extra else {},
        name="mixer",
    )(*operands)


def parts_of(value):
    high = value.astype(jnp.bfloat16)
    rest = value - high.astype(jnp.float32)
    middle = rest.astype(jnp.bfloat16)
    low = (rest - middle.astype(jnp.float32)).astype(jnp.bfloat16)
    return high, middle, low


def attend_kernel(groups, priors, tails, where_ref, lengths_ref, own_ref, *refs):
    sent = [g for g in groups if g]
    *refs, bias, peaks, totals = refs
    query_refs = dict(zip(sent, refs))
    prior_refs = refs[len(sent):len(sent) + priors]
    tail_refs = refs[len(sent) + priors:len(sent) + priors + tails]
    outs = refs[len(sent) + priors + tails:]
    if 0 in groups:
        out_ref, out_peak_ref, out_total_ref, *outs = outs
    sent_refs = dict(zip(sent, outs))
    count = own_ref.shape[1]
    width = own_ref.shape[2]
    heads = width // LANES
    scale = 1.0 / math.sqrt(LANES)
    index = where_ref[0]
    ends = bounds_of(lengths_ref)
    pivot = index == 1

    def mask(active, keys, first):
        row = lax.broadcasted_iota(jnp.int32, (count, keys), 0)
        source = first + lax.broadcasted_iota(jnp.int32, (count, keys), 1)
        for at, which in enumerate(active):
            place = (index + which) * count + row
            ok = (source <= place) & (source >= start_of(place, ends))
            bias[at * count:(at + 1) * count, 0:keys] = jnp.where(ok, 0.0, NEG)

    def queries_of(active, lanes):
        parts = [query_refs[g][:, lanes] if g else own_ref[0, :, lanes] for g in active]
        return jnp.concatenate(parts, axis=0)

    def store(active, lanes, mixed):
        for at, g in enumerate(active):
            value = mixed[at * count:(at + 1) * count]
            if g:
                sent_refs[g][0:count, lanes] = value.astype(sent_refs[g].dtype)
            else:
                out_ref[:, lanes] = value

    rate = scale * math.log2(math.e)

    def softmax(queries, keys, values):
        rows, extent = queries.shape[0], keys.shape[0]
        scores = lax.dot_general(queries, keys, (((1,), (1,)), ((), ())),
                                 preferred_element_type=jnp.float32)
        scores = scores + bias[0:rows, 0:extent]
        peak = jnp.maximum(jnp.max(scores, axis=1, keepdims=True), FLOOR)
        weights = jnp.exp2((scores - peak) * rate).astype(jnp.bfloat16)
        wide = jnp.concatenate([values, jnp.ones(values.shape, values.dtype)], axis=1)
        mixed = jnp.dot(weights, wide, preferred_element_type=jnp.float32)
        return mixed[:, :LANES], peak, mixed[:, LANES:]

    lane = lax.broadcasted_iota(jnp.int32, (1, LANES), 1)

    def several(one, rows):
        peaks[0:rows] = jnp.zeros((rows, LANES), jnp.float32)
        totals[0:rows] = jnp.zeros((rows, LANES), jnp.float32)
        for prior, begin in zip(prior_refs, range(0, heads, heads // priors)):
            def body(i, carry):
                peak_of, total_of = peaks[0:rows], totals[0:rows]
                for u in range(HEADS_AT_ONCE):
                    here = i * HEADS_AT_ONCE + u
                    h = begin + here
                    peak, total = one(pl.ds(pl.multiple_of(h * LANES, LANES), LANES), prior, here)
                    peak_of = jnp.where(lane == h, peak, peak_of)
                    total_of = jnp.where(lane == h, total, total_of)
                peaks[0:rows], totals[0:rows] = peak_of, total_of
                return carry
            lax.fori_loop(0, heads // priors // HEADS_AT_ONCE, body, 0)

    def run(active, before):
        mask(active, (1 + before) * count, (index - before) * count)

        def one(lanes, prior, h):
            keys, values = own_ref[1, :, lanes], own_ref[2, :, lanes]
            if before:
                here = pl.ds(pl.multiple_of(h * LANES, LANES), LANES)
                beside = pl.ds(pl.multiple_of(prior.shape[1] // 2 + h * LANES, LANES), LANES)
                keys = jnp.concatenate([prior[0:count, here], keys], axis=0)
                values = jnp.concatenate([prior[0:count, beside], values], axis=0)
            mixed, peak, total = softmax(queries_of(active, lanes), keys, values)
            store(active, lanes, mixed)
            return peak, total

        several(one, len(active) * count)

    @pl.when(pivot)
    def _():
        run(groups, 1)

    @pl.when(jnp.logical_not(pivot))
    def _():
        run([g for g in groups if g < 2], 0)

    if 0 in groups:
        out_peak_ref[...] = peaks[0:count]
        out_total_ref[...] = totals[0:count]
    for at, g in enumerate(groups):
        if g:
            rows = slice(at * count, (at + 1) * count)
            packed = jnp.zeros((count, LANES), jnp.float32)
            for n, piece in enumerate(parts_of(peaks[rows]) + parts_of(totals[rows])):
                piece = piece.astype(jnp.float32)
                packed = packed + (pltpu.roll(piece, n * SPREAD, 1) if n else piece)
            sent_refs[g][0:count, width:width + LANES] = packed.astype(sent_refs[g].dtype)

    for tail_ref, g in zip(tail_refs, sent):
        @pl.when(index == 0)
        def _():
            sent_refs[g][:, 0:width] = tail_ref[...]


def attend_part(index, lengths, blocks, groups, queries, priors, part, tails=()):
    slots, count, _ = blocks.shape
    width = queries[0].shape[1]
    rows = tails[0][0].shape[0] if tails else count
    whole = lambda i, *_: (0, 0)
    kind = queries[0].dtype
    out_shape = [jax.ShapeDtypeStruct((rows, width + LANES), kind) for _ in queries]
    out_specs = [pl.BlockSpec((rows, width + LANES), whole) for _ in queries]
    if 0 in groups:
        shapes = [(count, width), (count, LANES), (count, LANES)]
        out_shape = [pltpu.HBM(shape, jnp.float32) for shape in shapes] + out_shape
        out_specs = [pl.BlockSpec(shape, whole) for shape in shapes] + out_specs

    def tail_spec(at):
        return pl.BlockSpec((rows, width), lambda i, *_: (0, at))

    return pl.pallas_call(
        partial(attend_kernel, groups, len(priors), len(tails)),
        out_shape=out_shape,
        grid_spec=pltpu.PrefetchScalarGridSpec(
            num_scalar_prefetch=2,
            grid=(1,),
            in_specs=[pl.BlockSpec((slots, count, width), lambda i, *_: (0, 0, part))]
            + [pl.BlockSpec((count, width), whole) for _ in queries]
            + [pl.BlockSpec(prior.shape, whole) for prior in priors]
            + [tail_spec(at) for _, at in tails],
            out_specs=out_specs,
            scratch_shapes=[
                pltpu.VMEM((len(groups) * count, 2 * count), jnp.float32),
                pltpu.VMEM((len(groups) * count, LANES), jnp.float32),
                pltpu.VMEM((len(groups) * count, LANES), jnp.float32),
            ],
        ),
        compiler_params=pltpu.CompilerParams(vmem_limit_bytes=24 << 20),
        name="attend_part",
    )(index, lengths, blocks, *queries, *priors, *[array for array, _ in tails])


def merge_kernel(where_ref, own_ref, own_peak_ref, own_total_ref, near_ref, far_ref, *refs):
    out_ref = refs[-1]
    count, width = own_ref.shape
    index = where_ref[0]
    rate = math.log2(math.e) / math.sqrt(LANES)

    def stats(ref):
        packed = ref[:, width:width + LANES].astype(jnp.float32)
        pieces = [packed] + [pltpu.roll(packed, LANES - at * SPREAD, 1) for at in range(1, 6)]
        return pieces[0] + pieces[1] + pieces[2], pieces[3] + pieces[4] + pieces[5]

    @pl.when(index < 2)
    def _():
        part = 1.0 / jnp.where(own_total_ref[...] > 0.0, own_total_ref[...], 1.0)
        for h in range(width // LANES):
            lanes = slice(h * LANES, (h + 1) * LANES)
            out_ref[:, lanes] = (own_ref[:, lanes] * part[:, h:h + 1]).astype(out_ref.dtype)

    @pl.when(index >= 2)
    def _():
        both = index == 3
        own, total = own_peak_ref[...], own_total_ref[...]
        near, near_total = stats(near_ref)
        far, far_total = stats(far_ref)
        far = jnp.where(both, far, NEG)
        peak = jnp.maximum(own, jnp.maximum(near, far))
        own_part = jnp.exp2((own - peak) * rate)
        near_part = jnp.exp2((near - peak) * rate)
        far_part = jnp.exp2((far - peak) * rate)
        whole = own_part * total + near_part * near_total
        whole = whole + jnp.where(both, far_part * far_total, 0.0)
        whole = 1.0 / jnp.where(whole > 0.0, whole, 1.0)
        own_part, near_part, far_part = own_part * whole, near_part * whole, far_part * whole
        for h in range(width // LANES):
            lanes = slice(h * LANES, (h + 1) * LANES)
            mixed = own_ref[:, lanes] * own_part[:, h:h + 1]
            mixed = mixed + near_ref[:, lanes].astype(jnp.float32) * near_part[:, h:h + 1]
            mixed = mixed + jnp.where(
                both, far_ref[:, lanes].astype(jnp.float32) * far_part[:, h:h + 1], 0.0
            )
            out_ref[:, lanes] = mixed.astype(out_ref.dtype)


def merge_part(index, own, own_peak, own_total, near, far, first, full, held):
    count, width = own.shape
    whole = lambda i, *_: (0, 0)
    extra = () if held is None else (held,)
    return pl.pallas_call(
        merge_kernel,
        out_shape=jax.ShapeDtypeStruct((count, full), near.dtype),
        grid_spec=pltpu.PrefetchScalarGridSpec(
            num_scalar_prefetch=1,
            grid=(1,),
            in_specs=[
                pl.BlockSpec((count, width), whole),
                pl.BlockSpec((count, LANES), whole),
                pl.BlockSpec((count, LANES), whole),
                pl.BlockSpec((count, width + LANES), whole),
                pl.BlockSpec((count, width + LANES), whole),
            ]
            + [pl.BlockSpec(memory_space=pl.ANY)] * len(extra),
            out_specs=pl.BlockSpec((count, width), lambda i, *_: (0, first)),
        ),
        input_output_aliases={6: 0} if extra else {},
        name="merge_part",
    )(index, own, own_peak, own_total, near, far, *extra)


def layer_four(index, lengths, inputs, short_filter, base, blocks):
    reach = base.shape[1]
    width = blocks.shape[2]
    half = width // 2
    after = lax.optimization_barrier

    def queries(held, c):
        mine = held[0, :, c * half:(c + 1) * half]
        near = lax.ppermute(mine, "ctx", [(2, 1), (3, 2)])
        return near, lax.ppermute(mine, "ctx", [(3, 1)])

    def keys(held, c):
        cols = slice(c * half, (c + 1) * half)
        beside = jnp.concatenate([held[1, :, cols], held[2, :, cols]], axis=1)
        return lax.ppermute(beside, "ctx", [(0, 1)])

    def send(part, axis_pairs):
        return lax.ppermute(part, "ctx", axis_pairs)

    forward = [(0, 1), (1, 2), (2, 3)]
    near_a, far_a = queries(blocks, 0)
    prior_a = keys(blocks, 0)
    tail, message = mixer_tail(index, lengths, inputs, short_filter, reach, blocks, 1)
    moved = send(message, forward)
    held, near_a, tail = after((blocks, near_a, tail))
    near_b = send(held[0, :, half:], [(2, 1), (3, 2)])
    held, far_a, prior_a = after((held, far_a, prior_a))
    far_b = send(held[0, :, half:], [(3, 1)])
    *own_a, near_out, far_out = attend_part(
        index, lengths, blocks, (0, 1, 2), [near_a, far_a], [prior_a], 0, [(tail, 0), (tail, 1)]
    )
    near_in_a = send(near_out, forward)
    far_in_a = send(far_out, [(0, 1), (1, 3)])
    near_b, far_b, moved, _ = after((near_b, far_b, moved, far_out))
    *own_b, near_out, far_out = attend_part(
        index, lengths, blocks, (0, 1, 2), [near_b, far_b], [moved], 1
    )
    near_in_b = send(near_out, forward[1:])
    far_out, far_in_a = after((far_out, far_in_a))
    far_in_b = send(far_out, [(1, 3)])
    halo, far_in_a, _ = after((moved, far_in_a, near_out))
    hyena_out = mixer(
        index, lengths, inputs, short_filter, base, tail, [(halo, half), (far_in_a, 0)], half, half
    )
    far_in_a, near_in_a, _ = after((far_in_a, near_in_a, hyena_out))
    held = merge_part(index, *own_a, near_in_a, far_in_a, 0, width, None)
    tail, _ = after((tail, held))
    hyena_out = mixer(
        index, lengths, inputs, short_filter, base, tail, [(halo, 0), (near_in_a, 0)], 0, half, hyena_out
    )
    held, hyena_out = after((held, hyena_out))
    held = merge_part(index, *own_b, near_in_b, far_in_b, 1, width, held)
    return hyena_out, held


def attend_any(lengths, blocks, heads):
    count, width = blocks.shape[1:]
    depth = width // heads
    bounds = jnp.cumsum(lengths[0])[:-1]
    gathered = lax.all_gather(blocks[1:3], "ctx", axis=1, tiled=True)
    extent = gathered.shape[1]
    place = lax.axis_index("ctx") * count + jnp.arange(count, dtype=jnp.int32)
    source = jnp.arange(extent, dtype=jnp.int32)
    start = jnp.max(jnp.where(place[:, None] >= bounds[None, :], bounds[None, :], 0), axis=1)
    admit = (source[None, :] <= place[:, None]) & (source[None, :] >= start[:, None])
    queries = blocks[0].reshape(count, heads, depth)
    keys = gathered[0].reshape(extent, heads, depth)
    values = gathered[1].reshape(extent, heads, depth)
    scores = jnp.einsum("thd,shd->hts", queries, keys, preferred_element_type=jnp.float32)
    scores = jnp.where(admit[None], scores * (1.0 / math.sqrt(depth)), NEG)
    peak = jnp.max(scores, axis=2, keepdims=True)
    weights = jnp.where(admit[None], jnp.exp(scores - peak), 0.0)
    total = jnp.sum(weights, axis=2)
    mixed = jnp.einsum("hts,shd->htd", weights.astype(jnp.bfloat16), values,
                       preferred_element_type=jnp.float32)
    mixed = mixed / total[:, :, None]
    return mixed.transpose(1, 0, 2).reshape(count, width).astype(jnp.bfloat16)


def on_device(hyena_in, short_filter, long_filter, qkv, lengths):
    size = lax.axis_size("ctx")
    index = lax.axis_index("ctx").astype(jnp.int32).reshape(1)
    inputs = hyena_in[0].transpose(1, 0, 2)
    blocks = qkv[0].transpose(1, 0, 2)
    reach = long_filter.shape[0]
    taps = long_filter.astype(jnp.float32).T
    base = jnp.concatenate([taps[:, :1], taps[:, :0:-1]], axis=1)
    heads = H // lax.axis_size("tp")
    if size == 4:
        hyena_out, attn_out = layer_four(index, lengths, inputs, short_filter, base, blocks)
    else:
        (tail,) = mixer_tail(index, lengths, inputs, short_filter, reach)
        halo = lax.ppermute(tail, "ctx", [(i, i + 1) for i in range(size - 1)])
        hyena_out = mixer(
            index, lengths, inputs, short_filter, base, tail, [(halo, 0)], 0, inputs.shape[2]
        )
        attn_out = attend_any(lengths, blocks, heads)
    return (hyena_out[None], attn_out[None])


def solution(mesh):
    in_specs = (
        P(("groups", "dp"), "ctx", None, "tp"),
        P(None, None, "tp"),
        P(None, "tp"),
        P(("groups", "dp"), "ctx", None, "tp"),
        P(("groups", "dp"), None),
    )
    out_specs = (P(("groups", "dp"), "ctx", "tp"), P(("groups", "dp"), "ctx", "tp"))
    return jax.shard_map(
        on_device, mesh=mesh, in_specs=in_specs, out_specs=out_specs, check_vma=False
    )
```

```python
from functools import partial
import math

import jax
import jax.numpy as jnp
from jax import lax
from jax.experimental import pallas as pl
from jax.experimental.pallas import tpu as pltpu
from jax.sharding import PartitionSpec as P

H = 64
LANES = 128
ROWS = 32
TAIL_BLOCK = 1024
MIX_BLOCK = 512
HEADS_AT_ONCE = 8
MERGE_STEPS = 2
NEG = -1e30
FLOOR = -1e29


def bounds_of(lengths_ref):
    ends, total = [], 0
    for i in range(lengths_ref.shape[1] - 1):
        total = total + lengths_ref[0, i]
        ends.append(total)
    return ends


def start_of(places, ends):
    start = jnp.zeros(places.shape, jnp.int32)
    for end in ends:
        start = jnp.where(places >= end, end, start)
    return start


def filtered(line, offset, taps, keep, first, rows):
    outs = []
    for part in range(line.shape[0]):
        lanes = slice(part * LANES, (part + 1) * LANES)
        total = taps[0:1, lanes] * line[part, offset + first:offset + first + rows]
        for tap in range(1, keep.shape[0]):
            at = offset + first - tap
            total = total + taps[tap:tap + 1, lanes] * (
                line[part, at:at + rows] * keep[tap, first:first + rows]
            )
        outs.append(total)
    return jnp.concatenate(outs, axis=1)


def keep_taps(keep, anchor, ends):
    short, count, _ = keep.shape
    place = anchor + lax.broadcasted_iota(jnp.int32, (count, LANES), 0)
    start = start_of(place, ends)
    for tap in range(short):
        keep[tap] = (place - tap >= start).astype(jnp.float32)


def tail_kernel(where_ref, lengths_ref, gate_ref, value_ref, last_ref, taps_ref, *refs):
    *refs, line, keep, taps = refs
    extra = len(refs) // 2
    slab_refs, out_ref, message_refs = refs[:extra], refs[extra], refs[extra + 1:]
    count, width = gate_ref.shape
    reach = out_ref.shape[0] - 24
    first = count - reach
    short = taps_ref.shape[1]
    parts = line.shape[1]
    wide = parts * LANES

    @pl.when(pl.program_id(0) == 0)
    def _():
        keep_taps(keep, where_ref[0] * count, bounds_of(lengths_ref))

    taps[:, 0:short] = taps_ref[...].astype(jnp.float32)
    ends = [ref[ref.shape[0] - 16:].astype(jnp.float32)[8:] for ref in (gate_ref, last_ref, value_ref)]
    out_ref[reach:reach + 24] = jnp.concatenate(ends, axis=0).astype(out_ref.dtype)

    def one(i, carry):
        lanes = pl.ds(pl.multiple_of(i * wide, LANES), wide)
        for which, ref in enumerate((gate_ref, value_ref)):
            for part in range(parts):
                here = pl.ds(pl.multiple_of(i * wide + part * LANES, LANES), LANES)
                line[which, part] = ref[:, here].astype(jnp.float32)
        for at in range(first, count, ROWS):
            gate = filtered(line.at[0], 0, taps[0, :, lanes], keep, at, ROWS)
            value = filtered(line.at[1], 0, taps[2, :, lanes], keep, at, ROWS)
            out_ref[at - first:at - first + ROWS, lanes] = (gate * value).astype(out_ref.dtype)
        return carry

    lax.fori_loop(0, width // wide, one, 0)

    for slab_ref, message_ref in zip(slab_refs, message_refs):
        @pl.when(where_ref[0] == 0)
        def _():
            message_ref[0:count] = slab_ref[...]
            message_ref[count:] = jnp.zeros((reach + 24 - count, width), message_ref.dtype)

        @pl.when(where_ref[0] != 0)
        def _():
            message_ref[...] = out_ref[...]


def mixer_tail(index, lengths, inputs, short_filter, reach, blocks=None, slab=0):
    slots, count, width = inputs.shape
    block = min(width, 1024)
    short = short_filter.shape[1]
    rows = reach + 24
    each = width // 2 // block
    out = jax.ShapeDtypeStruct((rows, width), inputs.dtype)
    out_spec = pl.BlockSpec((rows, block), lambda i, *_: (0, i))
    extra = () if blocks is None else (blocks,)
    return pl.pallas_call(
        tail_kernel,
        out_shape=(out,) * (1 + len(extra)),
        grid_spec=pltpu.PrefetchScalarGridSpec(
            num_scalar_prefetch=2,
            grid=(width // block,),
            in_specs=[
                pl.BlockSpec((None, count, block), lambda i, *_: (0, 0, i)),
                pl.BlockSpec((None, count, block), lambda i, *_: (2, 0, i)),
                pl.BlockSpec((None, 16, block), lambda i, *_: (1, count // 16 - 1, i)),
                pl.BlockSpec((slots, short, block), lambda i, *_: (0, 0, i)),
            ]
            + [
                pl.BlockSpec(
                    (None, count, block), lambda i, *_: (1 + i // each, 0, slab * each + i % each)
                )
            ]
            * len(extra),
            out_specs=(out_spec,) * (1 + len(extra)),
            scratch_shapes=[
                pltpu.VMEM((2, 2, count, LANES), jnp.float32),
                pltpu.VMEM((short, count, LANES), jnp.float32),
                pltpu.VMEM((slots, 8, block), jnp.float32),
            ],
        ),
        name="mixer_tail",
    )(index, lengths, inputs, inputs, inputs, short_filter, *extra)


def mixer_kernel(halos, where_ref, lengths_ref, x1_ref, x2_ref, v_ref, taps_ref, base_ref, tail_ref, *refs):
    *halo_refs, out_ref, line, keep, taps, band_mask, band, window, gate = refs
    halo_refs = halo_refs[:halos]
    slots = taps_ref.shape[0]
    count, width = x2_ref.shape
    reach = base_ref.shape[1]
    rest = count - reach
    short = taps_ref.shape[1]
    parts = line.shape[1]
    wide = parts * LANES
    groups = band.shape[1] // count
    share = LANES // groups
    ends = bounds_of(lengths_ref)
    anchor = where_ref[0] * count

    @pl.when(pl.program_id(0) == 0)
    def _():
        keep_taps(keep, anchor, ends)
        row = lax.broadcasted_iota(jnp.int32, (count, LANES), 0)
        lane = lax.broadcasted_iota(jnp.int32, (count, LANES), 1)
        start = start_of(anchor + row, ends)
        under = jnp.where(row >= reach, row - reach, row)
        shift = jnp.where(row >= reach, reach, 0)
        source = anchor - reach + shift + lane
        older = (lane > under) & (source >= start)
        newer = (lane <= under) & (source + reach >= start)
        band_mask[:, 0:LANES] = older.astype(jnp.float32).astype(band_mask.dtype)
        band_mask[:, LANES:2 * LANES] = newer.astype(jnp.float32).astype(band_mask.dtype)
        window[reach + count:, :] = jnp.zeros((reach - rest, wide), window.dtype)

    taps[:, 0:short] = taps_ref[...].astype(jnp.float32)
    owner = lax.broadcasted_iota(jnp.int32, (1, LANES), 1) // share

    def halo(rows, lanes):
        total = halo_refs[0][rows, lanes]
        for ref in halo_refs[1:]:
            total = jnp.where(where_ref[0] == 1, ref[rows, lanes], total)
        return total

    def one(i, carry):
        lanes = pl.ds(pl.multiple_of(i * wide, LANES), wide)
        for part in range(parts):
            here = pl.ds(pl.multiple_of(i * wide + part * LANES, LANES), LANES)
            for slot, ref in enumerate((x1_ref, x2_ref, v_ref)):
                line[slot, part, 8:16] = halo(slice(reach, reach + 24), here).astype(jnp.float32)[
                    8 * slot:8 * slot + 8
                ]
                line[slot, part, 16:16 + ref.shape[0]] = ref[:, here].astype(jnp.float32)
        first = [filtered(line.at[slot], 16, taps[slot, :, lanes], keep, 0, rest) for slot in (0, 2)]
        window[0:reach] = halo(slice(0, reach), lanes)
        window[reach:reach + rest] = (first[0] * first[1]).astype(window.dtype)
        window[reach + rest:reach + count] = tail_ref[0:reach, lanes]
        for at in range(0, count, 48):
            gate[at:at + 48] = filtered(line.at[1], 16, taps[1, :, lanes], keep, at, 48)
        for part in range(wide // LANES):
            held = band.at[part]
            for g in range(groups):
                row = base_ref[pl.ds((i * (wide // LANES) + part) * groups + g, 1), :]
                circle = pltpu.roll(
                    jnp.broadcast_to(row, (reach, reach)), 0, 1, stride=1, stride_axis=0
                ).astype(band.dtype)
                for half in range(2):
                    cols = slice(half * LANES, (half + 1) * LANES)
                    held[g * reach:(g + 1) * reach, cols] = circle * band_mask[0:reach, cols]
                    held[groups * reach + g * rest:groups * reach + (g + 1) * rest, cols] = (
                        circle[0:rest] * band_mask[reach:count, cols]
                    )
            here = slice(part * LANES, (part + 1) * LANES)
            upper = jnp.dot(held[0:groups * reach, :], window[0:2 * reach, here],
                            preferred_element_type=jnp.float32)
            lower = jnp.dot(held[groups * reach:, :], window[reach:3 * reach, here],
                            preferred_element_type=jnp.float32)
            top, bottom = upper[0:reach], lower[0:rest]
            for g in range(1, groups):
                top = jnp.where(owner == g, upper[g * reach:(g + 1) * reach], top)
                bottom = jnp.where(owner == g, lower[g * rest:(g + 1) * rest], bottom)
            out_lanes = pl.ds(pl.multiple_of(i * wide + part * LANES, LANES), LANES)
            out_ref[0:reach, out_lanes] = (gate[0:reach, here] * top).astype(out_ref.dtype)
            out_ref[reach:count, out_lanes] = (gate[reach:count, here] * bottom).astype(out_ref.dtype)
        return carry

    lax.fori_loop(0, width // wide, one, 0)


def mixer(index, lengths, inputs, short_filter, base, tail, halos, first, cols, held=None):
    slots, count, width = inputs.shape
    filters, reach = base.shape
    rows = tail.shape[0]
    block = min(cols, 512)
    short = short_filter.shape[1]
    groups = LANES * filters // width
    wide = 2 * LANES
    start = first // block
    extra = () if held is None else (held,)
    received = [array for array, _ in halos]
    operands = (index, lengths, inputs, inputs, inputs, short_filter, base, tail, *received, *extra)

    def columns(at):
        at = at // block
        return pl.BlockSpec((rows, block), lambda i, *_: (0, at + i))

    return pl.pallas_call(
        partial(mixer_kernel, len(halos)),
        out_shape=jax.ShapeDtypeStruct((count, width), inputs.dtype),
        grid_spec=pltpu.PrefetchScalarGridSpec(
            num_scalar_prefetch=2,
            grid=(cols // block,),
            in_specs=[
                pl.BlockSpec((None, count - reach, block), lambda i, *_: (0, 0, start + i)),
                pl.BlockSpec((None, count, block), lambda i, *_: (1, 0, start + i)),
                pl.BlockSpec((None, count - reach, block), lambda i, *_: (2, 0, start + i)),
                pl.BlockSpec((slots, short, block), lambda i, *_: (0, 0, start + i)),
                pl.BlockSpec((filters * block // width, reach), lambda i, *_: (start + i, 0)),
                columns(first),
            ]
            + [columns(at) for _, at in halos]
            + [pl.BlockSpec(memory_space=pl.ANY)] * len(extra),
            out_specs=pl.BlockSpec((count, block), lambda i, *_: (0, start + i)),
            scratch_shapes=[
                pltpu.VMEM((slots, wide // LANES, 16 + count, LANES), jnp.float32),
                pltpu.VMEM((short, count, LANES), jnp.float32),
                pltpu.VMEM((slots, 8, block), jnp.float32),
                pltpu.VMEM((count, 2 * LANES), inputs.dtype),
                pltpu.VMEM((wide // LANES, groups * count, 2 * LANES), inputs.dtype),
                pltpu.VMEM((3 * reach, wide), inputs.dtype),
                pltpu.VMEM((count, wide), jnp.float32),
            ],
        ),
        input_output_aliases={len(operands) - 1: 0} if extra else {},
        name="mixer",
    )(*operands)


def in_hbm(array):
    return pltpu.with_memory_space_constraint(array, pltpu.HBM)


def parts_of(value):
    high = value.astype(jnp.bfloat16)
    rest = value - high.astype(jnp.float32)
    middle = rest.astype(jnp.bfloat16)
    low = (rest - middle.astype(jnp.float32)).astype(jnp.bfloat16)
    return high, middle, low


def attend_kernel(groups, priors, tails, where_ref, lengths_ref, own_ref, *refs):
    sent = [g for g in groups if g]
    *refs, bias, peaks, totals = refs
    query_refs = dict(zip(sent, refs))
    prior_refs = refs[len(sent):len(sent) + priors]
    tail_refs = refs[len(sent) + priors:len(sent) + priors + tails]
    outs = refs[len(sent) + priors + tails:]
    if 0 in groups:
        out_ref, out_peak_ref, out_total_ref, *outs = outs
    sent_refs = dict(zip(sent, outs))
    count = own_ref.shape[1]
    width = own_ref.shape[2]
    heads = width // LANES
    scale = 1.0 / math.sqrt(LANES)
    index = where_ref[0]
    ends = bounds_of(lengths_ref)
    pivot = index == 1

    def mask(active, keys, first):
        row = lax.broadcasted_iota(jnp.int32, (count, keys), 0)
        source = first + lax.broadcasted_iota(jnp.int32, (count, keys), 1)
        for at, which in enumerate(active):
            place = (index + which) * count + row
            ok = (source <= place) & (source >= start_of(place, ends))
            bias[at * count:(at + 1) * count, 0:keys] = jnp.where(ok, 0.0, NEG)

    def queries_of(active, lanes):
        parts = [query_refs[g][:, lanes] if g else own_ref[0, :, lanes] for g in active]
        return jnp.concatenate(parts, axis=0)

    def store(active, lanes, mixed):
        for at, g in enumerate(active):
            value = mixed[at * count:(at + 1) * count]
            if g:
                sent_refs[g][0:count, lanes] = value.astype(sent_refs[g].dtype)
            else:
                out_ref[:, lanes] = value

    rate = scale * math.log2(math.e)

    def softmax(queries, keys, values):
        rows, extent = queries.shape[0], keys.shape[0]
        scores = lax.dot_general(queries, keys, (((1,), (1,)), ((), ())),
                                 preferred_element_type=jnp.float32)
        scores = scores + bias[0:rows, 0:extent]
        peak = jnp.maximum(jnp.max(scores, axis=1, keepdims=True), FLOOR)
        peak = peak.astype(jnp.bfloat16).astype(jnp.float32)
        weights = jnp.exp2((scores - peak) * rate).astype(jnp.bfloat16)
        wide = jnp.concatenate([values, jnp.ones(values.shape, values.dtype)], axis=1)
        mixed = jnp.dot(weights, wide, preferred_element_type=jnp.float32)
        return mixed[:, :LANES], peak, mixed[:, LANES:]

    lane = lax.broadcasted_iota(jnp.int32, (1, LANES), 1)

    def several(one, rows):
        peaks[0:rows] = jnp.zeros((rows, LANES), jnp.float32)
        totals[0:rows] = jnp.zeros((rows, LANES), jnp.float32)
        for prior, begin in zip(prior_refs, range(0, heads, heads // priors)):
            def body(i, carry):
                peak_of, total_of = peaks[0:rows], totals[0:rows]
                for u in range(HEADS_AT_ONCE):
                    here = i * HEADS_AT_ONCE + u
                    h = begin + here
                    peak, total = one(pl.ds(pl.multiple_of(h * LANES, LANES), LANES), prior, here)
                    peak_of = jnp.where(lane == h, peak, peak_of)
                    total_of = jnp.where(lane == h, total, total_of)
                peaks[0:rows], totals[0:rows] = peak_of, total_of
                return carry
            lax.fori_loop(0, heads // priors // HEADS_AT_ONCE, body, 0)

    def run(active, before):
        mask(active, (1 + before) * count, (index - before) * count)

        def one(lanes, prior, h):
            keys, values = own_ref[1, :, lanes], own_ref[2, :, lanes]
            if before:
                here = pl.ds(pl.multiple_of(h * LANES, LANES), LANES)
                beside = pl.ds(pl.multiple_of(prior.shape[1] // 2 + h * LANES, LANES), LANES)
                keys = jnp.concatenate([prior[0:count, here], keys], axis=0)
                values = jnp.concatenate([prior[0:count, beside], values], axis=0)
            mixed, peak, total = softmax(queries_of(active, lanes), keys, values)
            store(active, lanes, mixed)
            return peak, total

        several(one, len(active) * count)

    @pl.when(pivot)
    def _():
        run(groups, 1)

    @pl.when(jnp.logical_not(pivot))
    def _():
        run([g for g in groups if g < 2], 0)

    if 0 in groups:
        out_peak_ref[...] = peaks[0:count]
        out_total_ref[...] = totals[0:count]
    for at, g in enumerate(groups):
        if g:
            rows = slice(at * count, (at + 1) * count)
            packed = peaks[rows]
            for n, piece in enumerate(parts_of(totals[rows])):
                packed = packed + pltpu.roll(piece.astype(jnp.float32), (n + 1) * heads, 1)
            tiles = [packed[8 * j:8 * j + 8] for j in range(count // 8)]
            for j in range(heads, len(tiles)):
                tiles[j - heads] = tiles[j - heads] + pltpu.roll(tiles[j], LANES // 2, 1)
            low = jnp.concatenate(tiles[:heads], axis=1)
            sent_refs[g][count:count + 8] = low.astype(sent_refs[g].dtype)

    for tail_ref, g in zip(tail_refs, sent):
        @pl.when(index == 0)
        def _():
            sent_refs[g][...] = tail_ref[...]


def attend_part(index, lengths, blocks, groups, queries, priors, part, tails=()):
    slots, count, _ = blocks.shape
    width = queries[0].shape[1]
    rows = count + 8
    whole = lambda i, *_: (0, 0)
    kind = queries[0].dtype
    out_shape = [jax.ShapeDtypeStruct((rows, width), kind) for _ in queries]
    out_specs = [pl.BlockSpec((rows, width), whole) for _ in queries]
    if 0 in groups:
        shapes = [(count, width), (count, LANES), (count, LANES)]
        out_shape = [pltpu.HBM(shape, jnp.float32) for shape in shapes] + out_shape
        out_specs = [pl.BlockSpec(shape, whole) for shape in shapes] + out_specs

    def tail_spec(at):
        return pl.BlockSpec((rows, width), lambda i, *_: (0, at))

    return pl.pallas_call(
        partial(attend_kernel, groups, len(priors), len(tails)),
        out_shape=out_shape,
        grid_spec=pltpu.PrefetchScalarGridSpec(
            num_scalar_prefetch=2,
            grid=(1,),
            in_specs=[pl.BlockSpec((slots, count, width), lambda i, *_: (0, 0, part))]
            + [pl.BlockSpec((count, width), whole) for _ in queries]
            + [pl.BlockSpec(prior.shape, whole) for prior in priors]
            + [tail_spec(at) for _, at in tails],
            out_specs=out_specs,
            scratch_shapes=[
                pltpu.VMEM((len(groups) * count, 2 * count), jnp.float32),
                pltpu.VMEM((len(groups) * count, LANES), jnp.float32),
                pltpu.VMEM((len(groups) * count, LANES), jnp.float32),
            ],
        ),
        compiler_params=pltpu.CompilerParams(vmem_limit_bytes=24 << 20),
        name="attend_part",
    )(index, lengths, in_hbm(blocks), *queries, *priors, *[array for array, _ in tails])


def merge_kernel(where_ref, own_ref, own_peak_ref, own_total_ref, near_ref, near_low_ref, far_ref,
                 far_low_ref, *refs):
    *_, out_ref, parts = refs
    count, width = own_ref.shape
    index = where_ref[0]
    rate = math.log2(math.e) / math.sqrt(LANES)
    step = pl.program_id(0)
    heads = near_low_ref.shape[1] // LANES

    def stats(ref):
        low = ref[...].astype(jnp.float32)
        tiles = [low[:, j % heads * LANES:(j % heads + 1) * LANES] for j in range(count // 8)]
        for j in range(heads, len(tiles)):
            tiles[j] = pltpu.roll(tiles[j], LANES // 2, 1)
        packed = jnp.concatenate(tiles, axis=0)
        total = pltpu.roll(packed, LANES - heads, 1) + pltpu.roll(packed, LANES - 2 * heads, 1)
        return packed, total + pltpu.roll(packed, LANES - 3 * heads, 1)

    @pl.when((step == 0) & (index < 2))
    def _():
        total = own_total_ref[...]
        parts[0] = 1.0 / jnp.where(total > 0.0, total, 1.0)

    @pl.when((step == 0) & (index >= 2))
    def _():
        both = index == 3
        held = lax.broadcasted_iota(jnp.int32, (count, LANES), 1) < heads
        own, total = own_peak_ref[...], own_total_ref[...]
        near, near_total = stats(near_low_ref)
        far, far_total = stats(far_low_ref)
        near = jnp.where(held, near, NEG)
        far = jnp.where(held & both, far, NEG)
        peak = jnp.maximum(own, jnp.maximum(near, far))
        own_part = jnp.exp2((own - peak) * rate)
        near_part = jnp.exp2((near - peak) * rate)
        far_part = jnp.exp2((far - peak) * rate)
        whole = own_part * total + jnp.where(held, near_part * near_total, 0.0)
        whole = whole + jnp.where(held & both, far_part * far_total, 0.0)
        whole = 1.0 / jnp.where(whole > 0.0, whole, 1.0)
        parts[0], parts[1], parts[2] = own_part * whole, near_part * whole, far_part * whole

    here = width // LANES
    turn = lax.rem(LANES - step * here, LANES)

    @pl.when(index < 2)
    def _():
        part = pltpu.roll(parts[0], turn, 1)
        for h in range(here):
            lanes = slice(h * LANES, (h + 1) * LANES)
            out_ref[:, lanes] = (own_ref[:, lanes] * part[:, h:h + 1]).astype(out_ref.dtype)

    @pl.when(index >= 2)
    def _():
        own_part, near_part, far_part = [pltpu.roll(parts[n], turn, 1) for n in range(3)]
        for h in range(here):
            lanes = slice(h * LANES, (h + 1) * LANES)
            mixed = own_ref[:, lanes] * own_part[:, h:h + 1]
            mixed = mixed + near_ref[:, lanes].astype(jnp.float32) * near_part[:, h:h + 1]
            mixed = mixed + jnp.where(
                index == 3, far_ref[:, lanes].astype(jnp.float32) * far_part[:, h:h + 1], 0.0
            )
            out_ref[:, lanes] = mixed.astype(out_ref.dtype)


def merge_part(index, own, own_peak, own_total, near, far, first, full, held):
    count, width = own.shape
    block = width // MERGE_STEPS
    start = first // block
    whole = lambda i, *_: (0, 0)
    extra = () if held is None else (held,)
    data = pl.BlockSpec((count, block), lambda i, *_: (0, i))
    low = pl.BlockSpec((8, width), lambda i, *_: (count // 8, 0))
    return pl.pallas_call(
        merge_kernel,
        out_shape=jax.ShapeDtypeStruct((count, full), near.dtype),
        grid_spec=pltpu.PrefetchScalarGridSpec(
            num_scalar_prefetch=1,
            grid=(MERGE_STEPS,),
            in_specs=[
                data,
                pl.BlockSpec((count, LANES), whole),
                pl.BlockSpec((count, LANES), whole),
                data,
                low,
                data,
                low,
            ]
            + [pl.BlockSpec(memory_space=pl.ANY)] * len(extra),
            out_specs=pl.BlockSpec((count, block), lambda i, *_: (0, start + i)),
            scratch_shapes=[pltpu.VMEM((3, count, LANES), jnp.float32)],
        ),
        input_output_aliases={8: 0} if extra else {},
        name="merge_part",
    )(index, own, own_peak, own_total, in_hbm(near), in_hbm(near), in_hbm(far), in_hbm(far), *extra)


def layer_four(index, lengths, inputs, short_filter, base, blocks):
    reach = base.shape[1]
    width = blocks.shape[2]
    half = width // 2
    after = lax.optimization_barrier

    def queries(held, c):
        mine = held[0, :, c * half:(c + 1) * half]
        near = lax.ppermute(mine, "ctx", [(2, 1), (3, 2)])
        return near, lax.ppermute(mine, "ctx", [(3, 1)])

    def keys(held, c):
        cols = slice(c * half, (c + 1) * half)
        beside = jnp.concatenate([held[1, :, cols], held[2, :, cols]], axis=1)
        return lax.ppermute(beside, "ctx", [(0, 1)])

    def send(part, axis_pairs):
        return lax.ppermute(part, "ctx", axis_pairs)

    forward = [(0, 1), (1, 2), (2, 3)]
    near_a, far_a = queries(blocks, 0)
    prior_a = keys(blocks, 0)
    tail, message = mixer_tail(index, lengths, inputs, short_filter, reach, blocks, 1)
    moved = send(message, forward)
    held, near_a, tail = after((blocks, near_a, tail))
    near_b = send(held[0, :, half:], [(2, 1), (3, 2)])
    held, far_a, prior_a = after((held, far_a, prior_a))
    far_b = send(held[0, :, half:], [(3, 1)])
    *own_a, near_out, far_out = attend_part(
        index, lengths, blocks, (0, 1, 2), [near_a, far_a], [prior_a], 0, [(tail, 0), (tail, 1)]
    )
    near_in_a = send(near_out, forward)
    far_in_a = send(far_out, [(0, 1), (1, 3)])
    near_b, far_b, moved, _ = after((near_b, far_b, moved, far_out))
    *own_b, near_out, far_out = attend_part(
        index, lengths, blocks, (0, 1, 2), [near_b, far_b], [moved], 1
    )
    near_in_b = send(near_out, forward[1:])
    far_out, far_in_a = after((far_out, far_in_a))
    far_in_b = send(far_out, [(1, 3)])
    halo, far_in_a, _ = after((moved, far_in_a, near_out))
    hyena_out = mixer(
        index, lengths, inputs, short_filter, base, tail, [(halo, half), (far_in_a, 0)], half, half
    )
    far_in_a, near_in_a, _ = after((far_in_a, near_in_a, hyena_out))
    held = merge_part(index, *own_a, near_in_a, far_in_a, 0, width, None)
    tail, _ = after((tail, held))
    hyena_out = mixer(
        index, lengths, inputs, short_filter, base, tail, [(halo, 0), (near_in_a, 0)], 0, half, hyena_out
    )
    held, hyena_out = after((held, hyena_out))
    held = merge_part(index, *own_b, near_in_b, far_in_b, half, width, held)
    return hyena_out, held


def attend_any(lengths, blocks, heads):
    count, width = blocks.shape[1:]
    depth = width // heads
    bounds = jnp.cumsum(lengths[0])[:-1]
    gathered = lax.all_gather(blocks[1:3], "ctx", axis=1, tiled=True)
    extent = gathered.shape[1]
    place = lax.axis_index("ctx") * count + jnp.arange(count, dtype=jnp.int32)
    source = jnp.arange(extent, dtype=jnp.int32)
    start = jnp.max(jnp.where(place[:, None] >= bounds[None, :], bounds[None, :], 0), axis=1)
    admit = (source[None, :] <= place[:, None]) & (source[None, :] >= start[:, None])
    queries = blocks[0].reshape(count, heads, depth)
    keys = gathered[0].reshape(extent, heads, depth)
    values = gathered[1].reshape(extent, heads, depth)
    scores = jnp.einsum("thd,shd->hts", queries, keys, preferred_element_type=jnp.float32)
    scores = jnp.where(admit[None], scores * (1.0 / math.sqrt(depth)), NEG)
    peak = jnp.max(scores, axis=2, keepdims=True)
    weights = jnp.where(admit[None], jnp.exp(scores - peak), 0.0)
    total = jnp.sum(weights, axis=2)
    mixed = jnp.einsum("hts,shd->htd", weights.astype(jnp.bfloat16), values,
                       preferred_element_type=jnp.float32)
    mixed = mixed / total[:, :, None]
    return mixed.transpose(1, 0, 2).reshape(count, width).astype(jnp.bfloat16)


def on_device(hyena_in, short_filter, long_filter, qkv, lengths):
    size = lax.axis_size("ctx")
    index = lax.axis_index("ctx").astype(jnp.int32).reshape(1)
    inputs = hyena_in[0].transpose(1, 0, 2)
    blocks = qkv[0].transpose(1, 0, 2)
    reach = long_filter.shape[0]
    taps = long_filter.astype(jnp.float32).T
    base = jnp.concatenate([taps[:, :1], taps[:, :0:-1]], axis=1)
    heads = H // lax.axis_size("tp")
    if size == 4:
        hyena_out, attn_out = layer_four(index, lengths, inputs, short_filter, base, blocks)
    else:
        (tail,) = mixer_tail(index, lengths, inputs, short_filter, reach)
        halo = lax.ppermute(tail, "ctx", [(i, i + 1) for i in range(size - 1)])
        hyena_out = mixer(
            index, lengths, inputs, short_filter, base, tail, [(halo, 0)], 0, inputs.shape[2]
        )
        attn_out = attend_any(lengths, blocks, heads)
    return (hyena_out[None], attn_out[None])


def solution(mesh):
    in_specs = (
        P(("groups", "dp"), "ctx", None, "tp"),
        P(None, None, "tp"),
        P(None, "tp"),
        P(("groups", "dp"), "ctx", None, "tp"),
        P(("groups", "dp"), None),
    )
    out_specs = (P(("groups", "dp"), "ctx", "tp"), P(("groups", "dp"), "ctx", "tp"))
    return jax.shard_map(
        on_device, mesh=mesh, in_specs=in_specs, out_specs=out_specs, check_vma=False
    )
```

```python
from functools import partial
import math

import jax
import jax.numpy as jnp
from jax import lax
from jax.experimental import pallas as pl
from jax.experimental.pallas import tpu as pltpu
from jax.sharding import PartitionSpec as P

H = 64
LANES = 128
ROWS = 32
TAIL_BLOCK = 1024
MIX_BLOCK = 512
HEADS_AT_ONCE = 8
MERGE_STEPS = 2
NEG = -1e30
FLOOR = -1e29


def bounds_of(lengths_ref):
    ends, total = [], 0
    for i in range(lengths_ref.shape[1] - 1):
        total = total + lengths_ref[0, i]
        ends.append(total)
    return ends


def start_of(places, ends):
    start = jnp.zeros(places.shape, jnp.int32)
    for end in ends:
        start = jnp.where(places >= end, end, start)
    return start


def filtered(line, offset, taps, keep, first, rows):
    outs = []
    for part in range(line.shape[0]):
        lanes = slice(part * LANES, (part + 1) * LANES)
        total = taps[0:1, lanes] * line[part, offset + first:offset + first + rows]
        for tap in range(1, keep.shape[0]):
            at = offset + first - tap
            total = total + taps[tap:tap + 1, lanes] * (
                line[part, at:at + rows] * keep[tap, first:first + rows]
            )
        outs.append(total)
    return jnp.concatenate(outs, axis=1)


def keep_taps(keep, anchor, ends):
    short, count, _ = keep.shape
    place = anchor + lax.broadcasted_iota(jnp.int32, (count, LANES), 0)
    start = start_of(place, ends)
    for tap in range(short):
        keep[tap] = (place - tap >= start).astype(jnp.float32)


def tail_kernel(where_ref, lengths_ref, gate_ref, value_ref, last_ref, taps_ref, *refs):
    *refs, line, keep, taps = refs
    extra = len(refs) // 2
    slab_refs, out_ref, message_refs = refs[:extra], refs[extra], refs[extra + 1:]
    count, width = gate_ref.shape
    reach = out_ref.shape[0] - 24
    first = count - reach
    short = taps_ref.shape[1]
    parts = line.shape[1]
    wide = parts * LANES

    @pl.when(pl.program_id(0) == 0)
    def _():
        keep_taps(keep, where_ref[0] * count, bounds_of(lengths_ref))

    taps[:, 0:short] = taps_ref[...].astype(jnp.float32)
    ends = [ref[ref.shape[0] - 16:].astype(jnp.float32)[8:] for ref in (gate_ref, last_ref, value_ref)]
    out_ref[reach:reach + 24] = jnp.concatenate(ends, axis=0).astype(out_ref.dtype)

    def one(i, carry):
        lanes = pl.ds(pl.multiple_of(i * wide, LANES), wide)
        for which, ref in enumerate((gate_ref, value_ref)):
            for part in range(parts):
                here = pl.ds(pl.multiple_of(i * wide + part * LANES, LANES), LANES)
                line[which, part] = ref[:, here].astype(jnp.float32)
        for at in range(first, count, ROWS):
            gate = filtered(line.at[0], 0, taps[0, :, lanes], keep, at, ROWS)
            value = filtered(line.at[1], 0, taps[2, :, lanes], keep, at, ROWS)
            out_ref[at - first:at - first + ROWS, lanes] = (gate * value).astype(out_ref.dtype)
        return carry

    lax.fori_loop(0, width // wide, one, 0)

    for slab_ref, message_ref in zip(slab_refs, message_refs):
        @pl.when(where_ref[0] == 0)
        def _():
            message_ref[0:count] = slab_ref[...]
            message_ref[count:] = jnp.zeros((reach + 24 - count, width), message_ref.dtype)

        @pl.when(where_ref[0] != 0)
        def _():
            message_ref[...] = out_ref[...]


def mixer_tail(index, lengths, inputs, short_filter, reach, blocks=None, slab=0):
    slots, count, width = inputs.shape
    block = min(width, 1024)
    short = short_filter.shape[1]
    rows = reach + 24
    each = width // 2 // block
    out = jax.ShapeDtypeStruct((rows, width), inputs.dtype)
    out_spec = pl.BlockSpec((rows, block), lambda i, *_: (0, i))
    extra = () if blocks is None else (blocks,)
    return pl.pallas_call(
        tail_kernel,
        out_shape=(out,) * (1 + len(extra)),
        grid_spec=pltpu.PrefetchScalarGridSpec(
            num_scalar_prefetch=2,
            grid=(width // block,),
            in_specs=[
                pl.BlockSpec((None, count, block), lambda i, *_: (0, 0, i)),
                pl.BlockSpec((None, count, block), lambda i, *_: (2, 0, i)),
                pl.BlockSpec((None, 16, block), lambda i, *_: (1, count // 16 - 1, i)),
                pl.BlockSpec((slots, short, block), lambda i, *_: (0, 0, i)),
            ]
            + [
                pl.BlockSpec(
                    (None, count, block), lambda i, *_: (1 + i // each, 0, slab * each + i % each)
                )
            ]
            * len(extra),
            out_specs=(out_spec,) * (1 + len(extra)),
            scratch_shapes=[
                pltpu.VMEM((2, 2, count, LANES), jnp.float32),
                pltpu.VMEM((short, count, LANES), jnp.float32),
                pltpu.VMEM((slots, 8, block), jnp.float32),
            ],
        ),
        name="mixer_tail",
    )(index, lengths, inputs, inputs, inputs, short_filter, *extra)


def mixer_kernel(halos, where_ref, lengths_ref, x1_ref, x2_ref, v_ref, taps_ref, base_ref, tail_ref, *refs):
    *halo_refs, out_ref, line, keep, taps, band_mask, band, window, gate = refs
    halo_refs = halo_refs[:halos]
    slots = taps_ref.shape[0]
    count, width = x2_ref.shape
    reach = base_ref.shape[1]
    rest = count - reach
    short = taps_ref.shape[1]
    parts = line.shape[1]
    wide = parts * LANES
    groups = band.shape[1] // count
    share = LANES // groups
    ends = bounds_of(lengths_ref)
    anchor = where_ref[0] * count

    @pl.when(pl.program_id(0) == 0)
    def _():
        keep_taps(keep, anchor, ends)
        row = lax.broadcasted_iota(jnp.int32, (count, LANES), 0)
        lane = lax.broadcasted_iota(jnp.int32, (count, LANES), 1)
        start = start_of(anchor + row, ends)
        under = jnp.where(row >= reach, row - reach, row)
        shift = jnp.where(row >= reach, reach, 0)
        source = anchor - reach + shift + lane
        older = (lane > under) & (source >= start)
        newer = (lane <= under) & (source + reach >= start)
        band_mask[:, 0:LANES] = older.astype(jnp.float32).astype(band_mask.dtype)
        band_mask[:, LANES:2 * LANES] = newer.astype(jnp.float32).astype(band_mask.dtype)
        window[reach + count:, :] = jnp.zeros((reach - rest, wide), window.dtype)

    taps[:, 0:short] = taps_ref[...].astype(jnp.float32)
    owner = lax.broadcasted_iota(jnp.int32, (1, LANES), 1) // share

    def halo(rows, lanes):
        total = halo_refs[0][rows, lanes]
        for ref in halo_refs[1:]:
            total = jnp.where(where_ref[0] == 1, ref[rows, lanes], total)
        return total

    def one(i, carry):
        lanes = pl.ds(pl.multiple_of(i * wide, LANES), wide)
        for part in range(parts):
            here = pl.ds(pl.multiple_of(i * wide + part * LANES, LANES), LANES)
            for slot, ref in enumerate((x1_ref, x2_ref, v_ref)):
                line[slot, part, 8:16] = halo(slice(reach, reach + 24), here).astype(jnp.float32)[
                    8 * slot:8 * slot + 8
                ]
                line[slot, part, 16:16 + ref.shape[0]] = ref[:, here].astype(jnp.float32)
        first = [filtered(line.at[slot], 16, taps[slot, :, lanes], keep, 0, rest) for slot in (0, 2)]
        window[0:reach] = halo(slice(0, reach), lanes)
        window[reach:reach + rest] = (first[0] * first[1]).astype(window.dtype)
        window[reach + rest:reach + count] = tail_ref[0:reach, lanes]
        for at in range(0, count, 48):
            gate[at:at + 48] = filtered(line.at[1], 16, taps[1, :, lanes], keep, at, 48)
        for part in range(wide // LANES):
            held = band.at[part]
            for g in range(groups):
                row = base_ref[pl.ds((i * (wide // LANES) + part) * groups + g, 1), :]
                circle = pltpu.roll(
                    jnp.broadcast_to(row, (reach, reach)), 0, 1, stride=1, stride_axis=0
                ).astype(band.dtype)
                for half in range(2):
                    cols = slice(half * LANES, (half + 1) * LANES)
                    held[g * reach:(g + 1) * reach, cols] = circle * band_mask[0:reach, cols]
                    held[groups * reach + g * rest:groups * reach + (g + 1) * rest, cols] = (
                        circle[0:rest] * band_mask[reach:count, cols]
                    )
            here = slice(part * LANES, (part + 1) * LANES)
            upper = jnp.dot(held[0:groups * reach, :], window[0:2 * reach, here],
                            preferred_element_type=jnp.float32)
            lower = jnp.dot(held[groups * reach:, :], window[reach:3 * reach, here],
                            preferred_element_type=jnp.float32)
            top, bottom = upper[0:reach], lower[0:rest]
            for g in range(1, groups):
                top = jnp.where(owner == g, upper[g * reach:(g + 1) * reach], top)
                bottom = jnp.where(owner == g, lower[g * rest:(g + 1) * rest], bottom)
            out_lanes = pl.ds(pl.multiple_of(i * wide + part * LANES, LANES), LANES)
            out_ref[0:reach, out_lanes] = (gate[0:reach, here] * top).astype(out_ref.dtype)
            out_ref[reach:count, out_lanes] = (gate[reach:count, here] * bottom).astype(out_ref.dtype)
        return carry

    lax.fori_loop(0, width // wide, one, 0)


def mixer(index, lengths, inputs, short_filter, base, tail, halos, first, cols, held=None):
    slots, count, width = inputs.shape
    filters, reach = base.shape
    rows = tail.shape[0]
    block = min(cols, 512)
    short = short_filter.shape[1]
    groups = LANES * filters // width
    wide = 2 * LANES
    start = first // block
    extra = () if held is None else (held,)
    received = [array for array, _ in halos]
    operands = (index, lengths, inputs, inputs, inputs, short_filter, base, tail, *received, *extra)

    def columns(at):
        at = at // block
        return pl.BlockSpec((rows, block), lambda i, *_: (0, at + i))

    return pl.pallas_call(
        partial(mixer_kernel, len(halos)),
        out_shape=jax.ShapeDtypeStruct((count, width), inputs.dtype),
        grid_spec=pltpu.PrefetchScalarGridSpec(
            num_scalar_prefetch=2,
            grid=(cols // block,),
            in_specs=[
                pl.BlockSpec((None, count - reach, block), lambda i, *_: (0, 0, start + i)),
                pl.BlockSpec((None, count, block), lambda i, *_: (1, 0, start + i)),
                pl.BlockSpec((None, count - reach, block), lambda i, *_: (2, 0, start + i)),
                pl.BlockSpec((slots, short, block), lambda i, *_: (0, 0, start + i)),
                pl.BlockSpec((filters * block // width, reach), lambda i, *_: (start + i, 0)),
                columns(first),
            ]
            + [columns(at) for _, at in halos]
            + [pl.BlockSpec(memory_space=pl.ANY)] * len(extra),
            out_specs=pl.BlockSpec((count, block), lambda i, *_: (0, start + i)),
            scratch_shapes=[
                pltpu.VMEM((slots, wide // LANES, 16 + count, LANES), jnp.float32),
                pltpu.VMEM((short, count, LANES), jnp.float32),
                pltpu.VMEM((slots, 8, block), jnp.float32),
                pltpu.VMEM((count, 2 * LANES), inputs.dtype),
                pltpu.VMEM((wide // LANES, groups * count, 2 * LANES), inputs.dtype),
                pltpu.VMEM((3 * reach, wide), inputs.dtype),
                pltpu.VMEM((count, wide), jnp.float32),
            ],
        ),
        input_output_aliases={len(operands) - 1: 0} if extra else {},
        name="mixer",
    )(*operands)


def in_hbm(array):
    return pltpu.with_memory_space_constraint(array, pltpu.HBM)


def parts_of(value):
    high = value.astype(jnp.bfloat16)
    rest = value - high.astype(jnp.float32)
    middle = rest.astype(jnp.bfloat16)
    low = (rest - middle.astype(jnp.float32)).astype(jnp.bfloat16)
    return high, middle, low


def attend_kernel(groups, priors, tails, where_ref, lengths_ref, own_ref, *refs):
    sent = [g for g in groups if g]
    *refs, bias, peaks, totals = refs
    query_refs = dict(zip(sent, refs))
    prior_refs = refs[len(sent):len(sent) + priors]
    tail_refs = refs[len(sent) + priors:len(sent) + priors + tails]
    outs = refs[len(sent) + priors + tails:]
    if 0 in groups:
        out_ref, out_peak_ref, out_total_ref, *outs = outs
    sent_refs = dict(zip(sent, outs))
    count = own_ref.shape[1]
    width = own_ref.shape[2]
    heads = width // LANES
    scale = 1.0 / math.sqrt(LANES)
    index = where_ref[0]
    ends = bounds_of(lengths_ref)
    pivot = index == 1

    def mask(active, keys, first):
        row = lax.broadcasted_iota(jnp.int32, (count, keys), 0)
        source = first + lax.broadcasted_iota(jnp.int32, (count, keys), 1)
        for at, which in enumerate(active):
            place = (index + which) * count + row
            ok = (source <= place) & (source >= start_of(place, ends))
            bias[at * count:(at + 1) * count, 0:keys] = jnp.where(ok, 0.0, NEG)

    def queries_of(active, lanes):
        parts = [query_refs[g][:, lanes] if g else own_ref[0, :, lanes] for g in active]
        return jnp.concatenate(parts, axis=0)

    def store(active, lanes, mixed):
        for at, g in enumerate(active):
            value = mixed[at * count:(at + 1) * count]
            if g:
                sent_refs[g][0:count, lanes] = value.astype(sent_refs[g].dtype)
            else:
                out_ref[:, lanes] = value

    rate = scale * math.log2(math.e)

    def softmax(queries, keys, values):
        rows, extent = queries.shape[0], keys.shape[0]
        scores = lax.dot_general(queries, keys, (((1,), (1,)), ((), ())),
                                 preferred_element_type=jnp.float32)
        scores = scores + bias[0:rows, 0:extent]
        peak = jnp.maximum(jnp.max(scores, axis=1, keepdims=True), FLOOR)
        peak = peak.astype(jnp.bfloat16).astype(jnp.float32)
        weights = jnp.exp2((scores - peak) * rate).astype(jnp.bfloat16)
        wide = jnp.concatenate([values, jnp.ones(values.shape, values.dtype)], axis=1)
        mixed = jnp.dot(weights, wide, preferred_element_type=jnp.float32)
        return mixed[:, :LANES], peak, mixed[:, LANES:]

    lane = lax.broadcasted_iota(jnp.int32, (1, LANES), 1)

    def several(one, rows):
        peaks[0:rows] = jnp.zeros((rows, LANES), jnp.float32)
        totals[0:rows] = jnp.zeros((rows, LANES), jnp.float32)
        for prior, begin in zip(prior_refs, range(0, heads, heads // priors)):
            def body(i, carry):
                peak_of, total_of = peaks[0:rows], totals[0:rows]
                for u in range(HEADS_AT_ONCE):
                    here = i * HEADS_AT_ONCE + u
                    h = begin + here
                    peak, total = one(pl.ds(pl.multiple_of(h * LANES, LANES), LANES), prior, here)
                    peak_of = jnp.where(lane == h, peak, peak_of)
                    total_of = jnp.where(lane == h, total, total_of)
                peaks[0:rows], totals[0:rows] = peak_of, total_of
                return carry
            lax.fori_loop(0, heads // priors // HEADS_AT_ONCE, body, 0)

    def run(active, before):
        mask(active, (1 + before) * count, (index - before) * count)

        def one(lanes, prior, h):
            keys, values = own_ref[1, :, lanes], own_ref[2, :, lanes]
            if before:
                here = pl.ds(pl.multiple_of(h * LANES, LANES), LANES)
                beside = pl.ds(pl.multiple_of(prior.shape[1] // 2 + h * LANES, LANES), LANES)
                keys = jnp.concatenate([prior[0:count, here], keys], axis=0)
                values = jnp.concatenate([prior[0:count, beside], values], axis=0)
            mixed, peak, total = softmax(queries_of(active, lanes), keys, values)
            store(active, lanes, mixed)
            return peak, total

        several(one, len(active) * count)

    @pl.when(pivot)
    def _():
        run(groups, 1)

    @pl.when(jnp.logical_not(pivot))
    def _():
        run([g for g in groups if g < 2], 0)

    if 0 in groups:
        out_peak_ref[...] = peaks[0:count]
        out_total_ref[...] = totals[0:count]
    for at, g in enumerate(groups):
        if g:
            rows = slice(at * count, (at + 1) * count)
            packed = peaks[rows]
            for n, piece in enumerate(parts_of(totals[rows])):
                packed = packed + pltpu.roll(piece.astype(jnp.float32), (n + 1) * heads, 1)
            tiles = [packed[8 * j:8 * j + 8] for j in range(count // 8)]
            for j in range(heads, len(tiles)):
                tiles[j - heads] = tiles[j - heads] + pltpu.roll(tiles[j], LANES // 2, 1)
            low = jnp.concatenate(tiles[:heads], axis=1)
            sent_refs[g][count:count + 8] = low.astype(sent_refs[g].dtype)

    for n, (tail_ref, g) in enumerate(zip(tail_refs, sent)):
        @pl.when(index == 0)
        def _():
            pltpu.sync_copy(tail_ref.at[:, n * width:(n + 1) * width], sent_refs[g])


def attend_part(index, lengths, blocks, groups, queries, priors, part, tails=()):
    slots, count, _ = blocks.shape
    width = queries[0].shape[1]
    rows = count + 8
    whole = lambda i, *_: (0, 0)
    kind = queries[0].dtype
    out_shape = [jax.ShapeDtypeStruct((rows, width), kind) for _ in queries]
    out_specs = [pl.BlockSpec((rows, width), whole) for _ in queries]
    if 0 in groups:
        shapes = [(count, width), (count, LANES), (count, LANES)]
        out_shape = [pltpu.HBM(shape, jnp.float32) for shape in shapes] + out_shape
        out_specs = [pl.BlockSpec(shape, whole) for shape in shapes] + out_specs

    return pl.pallas_call(
        partial(attend_kernel, groups, len(priors), len(tails)),
        out_shape=out_shape,
        grid_spec=pltpu.PrefetchScalarGridSpec(
            num_scalar_prefetch=2,
            grid=(1,),
            in_specs=[pl.BlockSpec((slots, count, width), lambda i, *_: (0, 0, part))]
            + [pl.BlockSpec((count, width), whole) for _ in queries]
            + [pl.BlockSpec(prior.shape, whole) for prior in priors]
            + [pl.BlockSpec(memory_space=pl.ANY) for _ in tails],
            out_specs=out_specs,
            scratch_shapes=[
                pltpu.VMEM((len(groups) * count, 2 * count), jnp.float32),
                pltpu.VMEM((len(groups) * count, LANES), jnp.float32),
                pltpu.VMEM((len(groups) * count, LANES), jnp.float32),
            ],
        ),
        compiler_params=pltpu.CompilerParams(vmem_limit_bytes=24 << 20),
        name="attend_part",
    )(index, lengths, in_hbm(blocks), *queries, *priors, *[in_hbm(tail) for tail in tails])


def merge_kernel(where_ref, own_ref, own_peak_ref, own_total_ref, near_ref, near_low_ref, far_ref,
                 far_low_ref, *refs):
    *_, out_ref, parts = refs
    count, width = own_ref.shape
    index = where_ref[0]
    rate = math.log2(math.e) / math.sqrt(LANES)
    step = pl.program_id(0)
    heads = near_low_ref.shape[1] // LANES

    def stats(ref):
        low = ref[...].astype(jnp.float32)
        tiles = [low[:, j % heads * LANES:(j % heads + 1) * LANES] for j in range(count // 8)]
        for j in range(heads, len(tiles)):
            tiles[j] = pltpu.roll(tiles[j], LANES // 2, 1)
        packed = jnp.concatenate(tiles, axis=0)
        total = pltpu.roll(packed, LANES - heads, 1) + pltpu.roll(packed, LANES - 2 * heads, 1)
        return packed, total + pltpu.roll(packed, LANES - 3 * heads, 1)

    @pl.when((step == 0) & (index < 2))
    def _():
        total = own_total_ref[...]
        parts[0] = 1.0 / jnp.where(total > 0.0, total, 1.0)

    @pl.when((step == 0) & (index >= 2))
    def _():
        both = index == 3
        held = lax.broadcasted_iota(jnp.int32, (count, LANES), 1) < heads
        own, total = own_peak_ref[...], own_total_ref[...]
        near, near_total = stats(near_low_ref)
        far, far_total = stats(far_low_ref)
        near = jnp.where(held, near, NEG)
        far = jnp.where(held & both, far, NEG)
        peak = jnp.maximum(own, jnp.maximum(near, far))
        own_part = jnp.exp2((own - peak) * rate)
        near_part = jnp.exp2((near - peak) * rate)
        far_part = jnp.exp2((far - peak) * rate)
        whole = own_part * total + jnp.where(held, near_part * near_total, 0.0)
        whole = whole + jnp.where(held & both, far_part * far_total, 0.0)
        whole = 1.0 / jnp.where(whole > 0.0, whole, 1.0)
        parts[0], parts[1], parts[2] = own_part * whole, near_part * whole, far_part * whole

    here = width // LANES
    turn = lax.rem(LANES - step * here, LANES)

    @pl.when(index < 2)
    def _():
        part = pltpu.roll(parts[0], turn, 1)
        for h in range(here):
            lanes = slice(h * LANES, (h + 1) * LANES)
            out_ref[:, lanes] = (own_ref[:, lanes] * part[:, h:h + 1]).astype(out_ref.dtype)

    @pl.when(index >= 2)
    def _():
        own_part, near_part, far_part = [pltpu.roll(parts[n], turn, 1) for n in range(3)]
        for h in range(here):
            lanes = slice(h * LANES, (h + 1) * LANES)
            mixed = own_ref[:, lanes] * own_part[:, h:h + 1]
            mixed = mixed + near_ref[:, lanes].astype(jnp.float32) * near_part[:, h:h + 1]
            mixed = mixed + jnp.where(
                index == 3, far_ref[:, lanes].astype(jnp.float32) * far_part[:, h:h + 1], 0.0
            )
            out_ref[:, lanes] = mixed.astype(out_ref.dtype)


def merge_part(index, own, own_peak, own_total, near, far, first, full, held):
    count, width = own.shape
    block = width // MERGE_STEPS
    start = first // block
    whole = lambda i, *_: (0, 0)
    extra = () if held is None else (held,)
    data = pl.BlockSpec((count, block), lambda i, *_: (0, i))
    low = pl.BlockSpec((8, width), lambda i, *_: (count // 8, 0))
    return pl.pallas_call(
        merge_kernel,
        out_shape=jax.ShapeDtypeStruct((count, full), near.dtype),
        grid_spec=pltpu.PrefetchScalarGridSpec(
            num_scalar_prefetch=1,
            grid=(MERGE_STEPS,),
            in_specs=[
                data,
                pl.BlockSpec((count, LANES), whole),
                pl.BlockSpec((count, LANES), whole),
                data,
                low,
                data,
                low,
            ]
            + [pl.BlockSpec(memory_space=pl.ANY)] * len(extra),
            out_specs=pl.BlockSpec((count, block), lambda i, *_: (0, start + i)),
            scratch_shapes=[pltpu.VMEM((3, count, LANES), jnp.float32)],
        ),
        input_output_aliases={8: 0} if extra else {},
        name="merge_part",
    )(index, own, own_peak, own_total, in_hbm(near), in_hbm(near), in_hbm(far), in_hbm(far), *extra)


def layer_four(index, lengths, inputs, short_filter, base, blocks):
    reach = base.shape[1]
    width = blocks.shape[2]
    half = width // 2
    after = lax.optimization_barrier

    def queries(held, c):
        mine = held[0, :, c * half:(c + 1) * half]
        near = lax.ppermute(mine, "ctx", [(2, 1), (3, 2)])
        return near, lax.ppermute(mine, "ctx", [(3, 1)])

    def keys(held, c):
        cols = slice(c * half, (c + 1) * half)
        beside = jnp.concatenate([held[1, :, cols], held[2, :, cols]], axis=1)
        return lax.ppermute(beside, "ctx", [(0, 1)])

    def send(part, axis_pairs):
        return lax.ppermute(part, "ctx", axis_pairs)

    forward = [(0, 1), (1, 2), (2, 3)]
    near_a, far_a = queries(blocks, 0)
    prior_a = keys(blocks, 0)
    tail, message = mixer_tail(index, lengths, inputs, short_filter, reach, blocks, 1)
    moved = send(message, forward)
    held, near_a, tail = after((blocks, near_a, tail))
    near_b = send(held[0, :, half:], [(2, 1), (3, 2)])
    held, far_a, prior_a = after((held, far_a, prior_a))
    far_b = send(held[0, :, half:], [(3, 1)])
    *own_a, near_out, far_out = attend_part(
        index, lengths, blocks, (0, 1, 2), [near_a, far_a], [prior_a], 0, [tail, tail]
    )
    near_in_a = send(near_out, forward)
    far_in_a = send(far_out, [(0, 1), (1, 3)])
    near_b, far_b, moved, _ = after((near_b, far_b, moved, far_out))
    *own_b, near_out, far_out = attend_part(
        index, lengths, blocks, (0, 1, 2), [near_b, far_b], [moved], 1
    )
    near_in_b = send(near_out, forward[1:])
    far_out, far_in_a = after((far_out, far_in_a))
    far_in_b = send(far_out, [(1, 3)])
    halo, far_in_a, _ = after((moved, far_in_a, near_out))
    hyena_out = mixer(
        index, lengths, inputs, short_filter, base, tail, [(halo, half), (far_in_a, 0)], half, half
    )
    far_in_a, near_in_a, _ = after((far_in_a, near_in_a, hyena_out))
    held = merge_part(index, *own_a, near_in_a, far_in_a, 0, width, None)
    tail, _ = after((tail, held))
    hyena_out = mixer(
        index, lengths, inputs, short_filter, base, tail, [(halo, 0), (near_in_a, 0)], 0, half, hyena_out
    )
    held, hyena_out = after((held, hyena_out))
    held = merge_part(index, *own_b, near_in_b, far_in_b, half, width, held)
    return hyena_out, held


def attend_any(lengths, blocks, heads):
    count, width = blocks.shape[1:]
    depth = width // heads
    bounds = jnp.cumsum(lengths[0])[:-1]
    gathered = lax.all_gather(blocks[1:3], "ctx", axis=1, tiled=True)
    extent = gathered.shape[1]
    place = lax.axis_index("ctx") * count + jnp.arange(count, dtype=jnp.int32)
    source = jnp.arange(extent, dtype=jnp.int32)
    start = jnp.max(jnp.where(place[:, None] >= bounds[None, :], bounds[None, :], 0), axis=1)
    admit = (source[None, :] <= place[:, None]) & (source[None, :] >= start[:, None])
    queries = blocks[0].reshape(count, heads, depth)
    keys = gathered[0].reshape(extent, heads, depth)
    values = gathered[1].reshape(extent, heads, depth)
    scores = jnp.einsum("thd,shd->hts", queries, keys, preferred_element_type=jnp.float32)
    scores = jnp.where(admit[None], scores * (1.0 / math.sqrt(depth)), NEG)
    peak = jnp.max(scores, axis=2, keepdims=True)
    weights = jnp.where(admit[None], jnp.exp(scores - peak), 0.0)
    total = jnp.sum(weights, axis=2)
    mixed = jnp.einsum("hts,shd->htd", weights.astype(jnp.bfloat16), values,
                       preferred_element_type=jnp.float32)
    mixed = mixed / total[:, :, None]
    return mixed.transpose(1, 0, 2).reshape(count, width).astype(jnp.bfloat16)


def on_device(hyena_in, short_filter, long_filter, qkv, lengths):
    size = lax.axis_size("ctx")
    index = lax.axis_index("ctx").astype(jnp.int32).reshape(1)
    inputs = hyena_in[0].transpose(1, 0, 2)
    blocks = qkv[0].transpose(1, 0, 2)
    reach = long_filter.shape[0]
    taps = long_filter.astype(jnp.float32).T
    base = jnp.concatenate([taps[:, :1], taps[:, :0:-1]], axis=1)
    heads = H // lax.axis_size("tp")
    if size == 4:
        hyena_out, attn_out = layer_four(index, lengths, inputs, short_filter, base, blocks)
    else:
        (tail,) = mixer_tail(index, lengths, inputs, short_filter, reach)
        halo = lax.ppermute(tail, "ctx", [(i, i + 1) for i in range(size - 1)])
        hyena_out = mixer(
            index, lengths, inputs, short_filter, base, tail, [(halo, 0)], 0, inputs.shape[2]
        )
        attn_out = attend_any(lengths, blocks, heads)
    return (hyena_out[None], attn_out[None])


def solution(mesh):
    in_specs = (
        P(("groups", "dp"), "ctx", None, "tp"),
        P(None, None, "tp"),
        P(None, "tp"),
        P(("groups", "dp"), "ctx", None, "tp"),
        P(("groups", "dp"), None),
    )
    out_specs = (P(("groups", "dp"), "ctx", "tp"), P(("groups", "dp"), "ctx", "tp"))
    return jax.shard_map(
        on_device, mesh=mesh, in_specs=in_specs, out_specs=out_specs, check_vma=False
    )
```
